256 devices in a mesh: frame: 32 (over z_hi, y, core), head: 8 (over z_lo, x).
Axes of the slice: x: 4, y: 4, z: 8 (z_hi: 4, z_lo: 2; z = z_hi * 2 + z_lo), core: 2. Of those that a mesh axis runs over, the one named last changes fastest.
Arguments:
- tokens: bfloat16 [8192, 3072], P('frame'), may hold values from -6 to 6
- w_qkv: bfloat16 [3, 3072, 3072], P(None, None, 'head'), may hold values from -0.109375 to 0.109375
- norm_gains: float32 [2, 3072], P(None, 'head'), may hold values from 0.8 to 2.5
- w_out: bfloat16 [3072, 3072], P('head'), may hold values from -0.15625 to 0.15625
- near_mask: int32 [64, 4], P('frame'), may hold values 0 or 1
- far_pattern: int32 [64, 64], P('frame'), may hold values from 0 to 1, as said below
- window: int32 [32], replicated, may hold values from 1 to 256, as said below
Outputs:
- layer_out: bfloat16 [8192, 3072], P('frame', 'head')
- checksum: float32 [8192], P('frame')
The draws below stay inside these ranges and needn't reach their ends.
Inputs may be any that keep to these rules, and one draw needn't show every extreme that they name: `far_pattern`: 0 or 1; entries whose two blocks lie in slabs less than two apart are never read. Entry d is the window for slabs d apart; entry 0 is 256.
All inputs are finite; a program needn't handle non-finite values. No bound on the sum of `near_mask` on one device may be relied on, other than what follows from the above.
Results may differ from the reference program's by a relative error of at most 0.015.
Values may be sent and summed in bfloat16 or wider, within the bound.
A program may use at most 128 MiB of HBM per device.

```python
import math
import jax
import jax.numpy as jnp
from jax import lax

D = 3072
HD = 128
HEADS = 24
TOK_DEV = 256
BLK = 128
NBLK = 2
TOKENS = 8192
QBLOCKS = 64


def draw_far_pattern(key, part):
    density_key = jax.random.fold_in(key, 11)
    grid_key = jax.random.fold_in(key, 12)
    slab_count = QBLOCKS // NBLK
    density = jax.random.randint(density_key, (slab_count,), 1, 9)
    density_rows = jnp.repeat(density, NBLK)
    draws_grid = jax.random.randint(grid_key, (QBLOCKS, QBLOCKS), 0, 8)
    return (draws_grid < density_rows[:, None]).astype(jnp.int32)


def draw_window(key, part):
    slab_count = QBLOCKS // NBLK
    base_draw = jax.random.randint(jax.random.fold_in(key, 21), (slab_count,), TOK_DEV // 4, TOK_DEV + 1)
    distance = jnp.arange(slab_count)
    narrowed = jnp.maximum(base_draw // (1 + distance // 8), 1)
    return jnp.where(distance == 0, TOK_DEV, narrowed).astype(jnp.int32)


def with_ends(values, key, smallest, top_value):
    extent = values.shape
    spot = [jax.random.randint(jax.random.fold_in(key, axis), (), 0, extent[axis]) for axis in range(len(extent))]
    values = values.at[tuple(spot)].set(smallest)
    longest = extent.index(max(extent))
    spot[longest] = (spot[longest] + 1) % extent[longest]
    return values.at[tuple(spot)].set(top_value)


def strengthened(entries, own_key, source, target, blocks, factor):
    def block_of(dim):
        return (jnp.arange(entries.shape[dim]) // (entries.shape[dim] // blocks)).reshape((-1,) + (1,) * (entries.ndim - 1 - dim))

    near = jax.random.permutation(own_key, blocks)[block_of(target)]
    other_side = (block_of(target) + blocks // 2) % blocks
    return jnp.where((block_of(source) == near) | (block_of(source) == other_side), factor * entries, entries)


def steps_of(own_key, dims, shards, least, largest):
    level = 1.0
    for axis_at, shards_of in shards:
        heights = jax.random.uniform(jax.random.fold_in(jax.random.fold_in(own_key, 6), axis_at), (shards_of,), jnp.float32, least / len(shards), largest / len(shards))
        level = level * jnp.repeat(jnp.exp(heights), dims[axis_at] // shards_of).reshape((-1,) + (1,) * (len(dims) - 1 - axis_at))
    return level


def gaussian(key, shape, width, bound, split=(), held_as=jnp.bfloat16):
    factor_of = steps_of(key, shape, split, -0.22, 0.18) if split else 1.0
    array = jax.random.normal(key, shape, jnp.float32) * width * factor_of
    return jnp.minimum(jnp.maximum(array, -bound), bound).astype(held_as)


def heavy_noise(key, shape, deviation, bound, pieces, heavy, dtype=jnp.bfloat16):
    drawn = deviation * jax.random.normal(key, shape, jnp.float32)
    if pieces:
        drawn = drawn * steps_of(key, shape, pieces, -0.22, 0.18)
    return jnp.clip(strengthened(drawn, jax.random.fold_in(key, 3), *heavy), -bound, bound).astype(dtype)


def setup_inputs(seed: int = 0) -> dict:
    arg_keys = jax.random.split(jax.random.key(seed), 8)
    tokens = gaussian(arg_keys[0], (TOKENS, D), 1.0, 6.0, ((0, 32),))
    w_qkv = gaussian(arg_keys[1], (3, D, HEADS * HD), D ** -0.5, 0.109375, ((2, 8),))
    norm_gains = jnp.clip(jnp.exp(math.log(2.5) - 1.13943427 * jax.random.uniform(arg_keys[2], (2, HEADS * HD), jnp.float32) ** steps_of(arg_keys[2], (2, HEADS * HD), ((1, 8),), -0.2, 0.2)), 0.8, 2.5)
    w_out = heavy_noise(arg_keys[3], (HEADS * HD, D), (HEADS * HD) ** -0.5, 0.15625, ((0, 8),), (0, 1, 8, 2.0))
    near_mask = with_ends((jax.random.randint(arg_keys[4], (QBLOCKS, 2 * NBLK), 0, 4) < 3).astype(jnp.int32), jax.random.fold_in(arg_keys[4], 1), 0, 1)
    far_pattern = draw_far_pattern(jax.random.fold_in(arg_keys[7], 71), 0)
    window = draw_window(jax.random.fold_in(arg_keys[7], 71), 0)
    return dict(tokens=tokens, w_qkv=w_qkv, norm_gains=norm_gains, w_out=w_out, near_mask=near_mask, far_pattern=far_pattern, window=window)


def normed_heads(values, gain_row):
    shaped = values.reshape(values.shape[0], -1, HD)
    factor = lax.rsqrt(lax.optimization_barrier(jnp.mean(shaped * shaped, axis=-1, keepdims=True)) + 1e-06)
    return shaped * factor * gain_row.reshape(-1, HD)

def reference(tokens, w_qkv, norm_gains, w_out, near_mask, far_pattern, window):
    query = jnp.dot(tokens, w_qkv[0], preferred_element_type=jnp.float32)
    key_full = jnp.dot(tokens, w_qkv[1], preferred_element_type=jnp.float32)
    value_full = jnp.dot(tokens, w_qkv[2], preferred_element_type=jnp.float32)
    queries = lax.optimization_barrier((normed_heads(query, norm_gains[0]) * HD ** (-0.5)).astype(jnp.bfloat16))
    keys_head = lax.optimization_barrier(normed_heads(key_full, norm_gains[1]).astype(jnp.bfloat16))
    values_head = lax.optimization_barrier(value_full.astype(jnp.bfloat16).reshape(TOKENS, -1, HD))
    keys_wide = keys_head.astype(jnp.float32)
    values_wide = values_head.astype(jnp.float32)
    n_blocks = TOK_DEV // BLK
    key_index = jnp.arange(TOKENS).astype(jnp.int32)
    key_slab = key_index // TOK_DEV
    key_pos = key_index % TOK_DEV
    key_block = key_index // BLK
    position = jnp.arange(TOK_DEV).astype(jnp.int32)

    def one_slab(slab_id):
        query_rows = lax.dynamic_slice_in_dim(queries, slab_id * TOK_DEV, TOK_DEV, 0).astype(jnp.float32)
        far_rows = lax.dynamic_slice_in_dim(far_pattern, slab_id * n_blocks, n_blocks, 0)
        near_rows = lax.dynamic_slice_in_dim(near_mask, slab_id * n_blocks, n_blocks, 0)
        distance = jnp.abs(key_slab - slab_id)
        key_side = jnp.where(key_slab < slab_id, 0, 1).astype(jnp.int32)
        near_cols = (key_side * n_blocks + key_pos // BLK).astype(jnp.int32)
        far_sel = far_rows[:, key_block]
        near_sel = near_rows[:, near_cols]
        chosen = jnp.where(distance == 0, 1, jnp.where(distance == 1, near_sel, far_sel))
        chosen = jnp.repeat(chosen, BLK, axis=0)
        key_limit = window[distance]
        allowed = (chosen > 0) & (jnp.abs(position[:, None] - key_pos[None, :]) < key_limit[None, :])
        scores = jnp.einsum('qhd,khd->hqk', query_rows, keys_wide)
        weights = jnp.where(allowed[None], jnp.exp(scores), 0.0)
        total = lax.optimization_barrier(jnp.sum(weights, axis=-1))
        rounded = lax.optimization_barrier(weights.astype(jnp.bfloat16)).astype(jnp.float32)
        numer = jnp.einsum('hqk,khd->qhd', rounded, values_wide)
        return (numer / total.T[:, :, None]).reshape(TOK_DEV, -1).astype(jnp.bfloat16)
    slab_ids = jnp.arange(TOKENS // TOK_DEV).astype(jnp.int32)
    attended = lax.map(one_slab, slab_ids).reshape(TOKENS, -1)
    full = jnp.dot(attended, w_out, preferred_element_type=jnp.float32)
    checksum = lax.optimization_barrier(jnp.sum(full, axis=1)) * D ** (-0.5)
    return (full.astype(jnp.bfloat16), checksum)
```

```python
import jax
import jax.numpy as jnp
from jax import lax
from jax.experimental import pallas as pl
from jax.experimental.pallas import tpu as pltpu
from jax.sharding import PartitionSpec as P

D = 3072
HD = 128
BLK = 128
SLAB = 256
HL = 3
COLS = HL * HD
MESH = pl.DeviceIdType.MESH
BF = jnp.bfloat16
F32 = jnp.float32
LOG2E = 1.4426950408889634
OROWS = BLK + 16
CUT = 80
NT = (((1,), (1,)), ((), ()))


def layer_kernel(
    tok_hbm,
    w_hbm,
    wo_hbm,
    gains_ref,
    thr_ref,
    out_ref,
    cs_ref,
    tok,
    wkv,
    wq,
    wo,
    kv,
    qb,
    tbuf,
    texp,
    dist,
    pbuf,
    num,
    tot,
    osend,
    orel_a,
    orel_b,
    ofin,
    xf,
    xopp,
    xrel,
    xs,
    xfin,
    zs,
    zr,
    csb,
    lsem,
    kss,
    krs,
    qss,
    qrs,
    tss,
    trs,
    oss,
    ors,
    xss,
    xrs,
    css,
    crs,
):
    f = lax.axis_index("frame")
    g = lax.axis_index("head")
    zh, y, c = f // 8, (f // 2) % 4, f % 2
    zl, x = g // 4, g % 4

    def at_y(step):
        return (zh * 8 + ((y + step) % 4) * 2 + c, g)

    def at_z(step):
        return (((zh + step) % 4) * 8 + y * 2 + c, g)

    def at_x(step):
        return (f, zl * 4 + (x + step) % 4)

    core = (zh * 8 + y * 2 + (1 - c), g)
    zlo = (f, (1 - zl) * 4 + x)

    started = []

    def send(src, dst, ssem, rsem, dev):
        copy = pltpu.make_async_remote_copy(
            src_ref=src, dst_ref=dst, send_sem=ssem, recv_sem=rsem, device_id=dev, device_id_type=MESH
        )
        copy.start()
        started.append(copy)
        return copy

    def fetch(src, dst, i):
        copy = pltpu.make_async_copy(src, dst, lsem.at[i])
        copy.start()
        return copy

    tok_in = fetch(tok_hbm, tok, 0)
    kv_in = []
    for h in range(HL):
        hs = pl.ds(h * HD, HD)
        kv_in.append(
            (
                fetch(w_hbm.at[1, :, hs], wkv.at[h, :, pl.ds(0, HD)], 1 + 2 * h),
                fetch(w_hbm.at[2, :, hs], wkv.at[h, :, pl.ds(HD, HD)], 2 + 2 * h),
            )
        )
        if h == 0:
            q_in = fetch(w_hbm.at[0], wq, 7)
    wo_in = fetch(wo_hbm, wo, 8)

    barrier = pltpu.get_barrier_semaphore()
    peers = [at_y(1), at_y(3), core, at_z(1), at_z(3), at_z(2)]
    peers += [(f, (g + k) % 8) for k in range(1, 8)]
    for peer in peers:
        pl.semaphore_signal(barrier, inc=1, device_id=peer, device_id_type=MESH)

    def make_kv(h):
        for copy in kv_in[h]:
            copy.wait()
        both = jnp.dot(tok[...], wkv[h], preferred_element_type=F32)
        key = both[:, :HD]
        factor = lax.rsqrt(jnp.mean(key * key, axis=1, keepdims=True) + 1e-06)
        gain = gains_ref[1:2, h * HD : (h + 1) * HD]
        kv[h, 0, :, 0:HD] = (key * factor * gain).astype(BF)
        kv[h, 0, :, HD : 2 * HD] = both[:, HD:].astype(BF)

    def make_q():
        q_in.wait()
        whole = jnp.dot(tok[...], wq[...], preferred_element_type=F32)
        for h in range(HL):
            query = whole[:, h * HD : (h + 1) * HD]
            factor = lax.rsqrt(jnp.mean(query * query, axis=1, keepdims=True) + 1e-06)
            gain = gains_ref[0:1, h * HD : (h + 1) * HD] * (HD**-0.5 * LOG2E)
            qb[h, 0] = (query * factor * gain).astype(BF)

    top, low = pl.ds(0, BLK), pl.ds(BLK, BLK)
    kcopy, qcopy = {}, {}

    def send_kv(h):
        own = kv.at[h, 0]
        kcopy[h, "R"] = send(own, kv.at[h, 1], kss.at[h, 0], krs.at[h, 0], at_y(1))
        kcopy[h, "L"] = send(own, kv.at[h, 2], kss.at[h, 1], krs.at[h, 1], at_y(3))
        kcopy[h, "c0"] = send(own, kv.at[h, 4], kss.at[h, 2], krs.at[h, 2], core)

    def relay_kv(h):
        kcopy[h, "R"].wait_recv()
        kcopy[h, "RR"] = send(
            kv.at[h, 1, top], kv.at[h, 3, top], kss.at[h, 3], krs.at[h, 3], at_y(1)
        )
        kcopy[h, "c1"] = send(kv.at[h, 1], kv.at[h, 5], kss.at[h, 4], krs.at[h, 4], core)
        kcopy[h, "L"].wait_recv()
        kcopy[h, "LL"] = send(
            kv.at[h, 2, low], kv.at[h, 3, low], kss.at[h, 5], krs.at[h, 5], at_y(3)
        )
        kcopy[h, "c2"] = send(kv.at[h, 2], kv.at[h, 6], kss.at[h, 6], krs.at[h, 6], core)

    def last_kv(h):
        kcopy[h, "RR"].wait_recv()
        kcopy[h, "LL"].wait_recv()
        kcopy[h, "c3"] = send(kv.at[h, 3], kv.at[h, 7], kss.at[h, 7], krs.at[h, 7], core)

    def arrived_kv(h):
        for name in ("c0", "c1", "c2", "c3"):
            kcopy[h, name].wait_recv()

    def send_q(h):
        own = qb.at[h, 0]
        qcopy[h, "R"] = send(own, qb.at[h, 1], qss.at[h, 0], qrs.at[h, 0], at_z(1))
        qcopy[h, "L"] = send(own, qb.at[h, 2], qss.at[h, 1], qrs.at[h, 1], at_z(3))

    def relay_q(h):
        qcopy[h, "R"].wait_recv()
        qcopy[h, "RR"] = send(
            qb.at[h, 1, top], qb.at[h, 3, top], qss.at[h, 2], qrs.at[h, 2], at_z(1)
        )
        qcopy[h, "L"].wait_recv()
        qcopy[h, "LL"] = send(
            qb.at[h, 2, low], qb.at[h, 3, low], qss.at[h, 3], qrs.at[h, 3], at_z(3)
        )

    def arrived_q(h):
        qcopy[h, "RR"].wait_recv()
        qcopy[h, "LL"].wait_recv()

    tok_in.wait()
    make_kv(0)
    pl.semaphore_wait(barrier, len(peers))
    send_kv(0)
    tcopy = [
        send(thr_ref, tbuf.at[1], tss.at[0], trs.at[0], at_z(1)),
        send(thr_ref, tbuf.at[2], tss.at[1], trs.at[1], at_z(3)),
        send(thr_ref, tbuf.at[3], tss.at[2], trs.at[2], at_z(2)),
    ]
    make_q()
    for h in range(HL):
        send_q(h)
    make_kv(1)
    send_kv(1)
    make_kv(2)
    send_kv(2)

    row = lax.broadcasted_iota(jnp.int32, (BLK, SLAB), 0)
    col = lax.broadcasted_iota(jnp.int32, (BLK, SLAB), 1)
    for rh in range(2):
        dist[rh] = jnp.abs(row + rh * BLK - col).astype(F32)
    tbuf[0] = thr_ref[...]
    for copy in tcopy:
        copy.wait_recv()
    table = tbuf[...].reshape(4 * 8, 128).astype(BF)
    half = (col >= BLK).astype(jnp.int32)
    for j in range(8):
        slab = zh * 8 + ((y + (0, 3, 1, 2)[j % 4]) % 4) * 2 + (c if j < 4 else 1 - c)
        pick = (row == half + slab * 2).astype(F32).astype(BF)
        texp[j] = jnp.dot(table, pick, preferred_element_type=F32)

    for h in range(HL):
        relay_kv(h)
        relay_q(h)
        if h >= 1:
            last_kv(h - 1)

    ocopy = {}

    def attend(s):
        rh, h = s // HL, s % HL
        queries = qb[h, :, rh * BLK : (rh + 1) * BLK, :].reshape(4 * BLK, HD)

        def scores(j, carry):
            raw = lax.dot_general(queries, kv[h, j, :, 0:HD], NT, preferred_element_type=F32)
            away = dist[rh]
            cols = pl.ds(pl.multiple_of(j * SLAB, SLAB), SLAB)
            for q in range(4):
                limit = texp[j, q * 8 + rh : q * 8 + rh + 1, :]
                weight = jnp.where(away < limit, jnp.exp2(raw[q * BLK : (q + 1) * BLK]), 0.0)
                pbuf[q * BLK : (q + 1) * BLK, cols] = weight.astype(BF)
            return carry

        lax.fori_loop(0, 8, scores, 0)
        values = kv[h, :, :, HD : 2 * HD].reshape(8 * SLAB, HD)
        values = jnp.concatenate([values, jnp.ones((8 * SLAB, HD), BF)], axis=1)
        result = jnp.dot(pbuf[...], values, preferred_element_type=F32)
        num[s] = result[:BLK, :HD]
        tot[s] = result[:BLK, HD:]
        for q in (1, 2, 3):
            part = result[q * BLK : (q + 1) * BLK]
            osend[s, q - 1, 0:BLK, :] = part[:, :HD].astype(BF)
            osend[s, q - 1, BLK:OROWS, :] = part[:, HD:].T[0:16].astype(BF)
        first, last = pl.ds(0, CUT), pl.ds(CUT, OROWS - CUT)
        ocopy[s, "RR"] = send(
            osend.at[s, 2, first], orel_a.at[s], oss.at[s, 0], ors.at[s, 0], at_z(1)
        )
        ocopy[s, "LL"] = send(
            osend.at[s, 2, last], orel_b.at[s], oss.at[s, 1], ors.at[s, 1], at_z(3)
        )
        ocopy[s, "R1"] = send(
            osend.at[s, 1, last], ofin.at[s, 0, last], oss.at[s, 2], ors.at[s, 2], at_z(1)
        )
        ocopy[s, "L0"] = send(
            osend.at[s, 0, first], ofin.at[s, 1, first], oss.at[s, 3], ors.at[s, 3], at_z(3)
        )

    def relay_o(s):
        first, last = pl.ds(0, CUT), pl.ds(CUT, OROWS - CUT)
        ocopy[s, "RR"].wait_recv()
        osend[s, 1, 0:CUT, :] = (
            osend[s, 1, 0:CUT, :].astype(F32) + orel_a[s].astype(F32)
        ).astype(BF)
        ocopy[s, "R0"] = send(
            osend.at[s, 1, first], ofin.at[s, 0, first], oss.at[s, 4], ors.at[s, 4], at_z(1)
        )
        ocopy[s, "LL"].wait_recv()
        osend[s, 0, CUT:OROWS, :] = (
            osend[s, 0, CUT:OROWS, :].astype(F32) + orel_b[s].astype(F32)
        ).astype(BF)
        ocopy[s, "L1"] = send(
            osend.at[s, 0, last], ofin.at[s, 1, last], oss.at[s, 5], ors.at[s, 5], at_z(3)
        )

    def attended_of(s):
        for name in ("R0", "R1", "L0", "L1"):
            ocopy[s, name].wait_recv()
        more = ofin[s, 0].astype(F32) + ofin[s, 1].astype(F32)
        numer = num[s] + more[:BLK]
        strip = more[BLK:OROWS]
        total = tot[s] + jnp.concatenate([strip] * 8, axis=0).T
        return (numer / total).astype(BF)

    xcopy, ccopy = {}, {}

    def project(rh):
        rows = jnp.concatenate([attended_of(rh * HL + h) for h in range(HL)], axis=1)

        def share(side, step):
            at = (side * 4 + (x + step) % 4) * COLS
            block = wo[:, pl.ds(pl.multiple_of(at, HD), COLS)]
            return jnp.dot(rows, block, preferred_element_type=F32)

        opp = [share(0, 2), share(1, 2)]
        for side in range(2):
            xopp[rh, side] = opp[side].astype(BF)
        xcopy[rh, "RR"] = send(
            xopp.at[rh, 0], xrel.at[rh, 0], xss.at[rh, 0], xrs.at[rh, 0], at_x(1)
        )
        xcopy[rh, "LL"] = send(
            xopp.at[rh, 1], xrel.at[rh, 1], xss.at[rh, 1], xrs.at[rh, 1], at_x(3)
        )
        sums = opp[0] + opp[1]
        r1 = share(1, 1)
        xs[rh, 0, 1] = r1.astype(BF)
        xcopy[rh, "R1"] = send(
            xs.at[rh, 0, 1], xfin.at[rh, 0, 1], xss.at[rh, 2], xrs.at[rh, 2], at_x(1)
        )
        l0 = share(0, 3)
        xs[rh, 1, 0] = l0.astype(BF)
        xcopy[rh, "L0"] = send(
            xs.at[rh, 1, 0], xfin.at[rh, 1, 0], xss.at[rh, 3], xrs.at[rh, 3], at_x(3)
        )
        r0 = share(0, 1)
        xf[rh, 2] = r0
        l1 = share(1, 3)
        xf[rh, 3] = l1
        sums = sums + r1 + l0 + r0 + l1
        for side in range(2):
            mine = share(side, 0)
            xf[rh, side] = mine
            sums = sums + mine
        turned = (sums[:, :HD] + sums[:, HD : 2 * HD] + sums[:, 2 * HD :]).T
        line = jnp.sum(turned, axis=0, keepdims=True) * D ** (-0.5)
        csb[rh, g] = jnp.broadcast_to(line, (8, BLK))
        for k in range(1, 8):
            ccopy[rh, k] = send(
                csb.at[rh, g], csb.at[rh, g], css.at[rh, k], crs.at[rh, k], (f, (g + k) % 8)
            )

    def relay_x(rh):
        xcopy[rh, "RR"].wait_recv()
        xs[rh, 0, 0] = (xf[rh, 2] + xrel[rh, 0].astype(F32)).astype(BF)
        xcopy[rh, "R0"] = send(
            xs.at[rh, 0, 0], xfin.at[rh, 0, 0], xss.at[rh, 4], xrs.at[rh, 4], at_x(1)
        )
        xcopy[rh, "LL"].wait_recv()
        xs[rh, 1, 1] = (xf[rh, 3] + xrel[rh, 1].astype(F32)).astype(BF)
        xcopy[rh, "L1"] = send(
            xs.at[rh, 1, 1], xfin.at[rh, 1, 1], xss.at[rh, 5], xrs.at[rh, 5], at_x(3)
        )

    def cross(rh):
        for name in ("R0", "R1", "L0", "L1"):
            xcopy[rh, name].wait_recv()
        other = 1 - zl
        zs[rh] = (
            xf[rh, other] + xfin[rh, 0, other].astype(F32) + xfin[rh, 1, other].astype(F32)
        ).astype(BF)
        xcopy[rh, "z"] = send(zs.at[rh], zr.at[rh], xss.at[rh, 6], xrs.at[rh, 6], zlo)

    def finish(rh):
        held = xf[rh, zl] + xfin[rh, 0, zl].astype(F32) + xfin[rh, 1, zl].astype(F32)
        xcopy[rh, "z"].wait_recv()
        out_ref[rh * BLK : (rh + 1) * BLK, :] = (held + zr[rh].astype(F32)).astype(BF)
        for k in range(1, 8):
            pltpu.make_async_remote_copy(
                src_ref=csb.at[rh, (g + 8 - k) % 8],
                dst_ref=csb.at[rh, (g + 8 - k) % 8],
                send_sem=css.at[rh, k],
                recv_sem=crs.at[rh, k],
                device_id=(f, (g + k) % 8),
                device_id_type=MESH,
            ).wait_recv()
        total = csb[rh, 0]
        for k in range(1, 8):
            total = total + csb[rh, k]
        cs_ref[rh] = total

    arrived_kv(0)
    arrived_q(0)
    attend(0)
    last_kv(2)
    arrived_kv(1)
    arrived_q(1)
    attend(1)
    relay_o(0)
    arrived_kv(2)
    arrived_q(2)
    attend(2)
    relay_o(1)
    attend(3)
    relay_o(2)
    attend(4)
    relay_o(3)
    wo_in.wait()
    project(0)
    attend(5)
    relay_o(4)
    relay_x(0)
    relay_o(5)
    cross(0)
    project(1)
    finish(0)
    relay_x(1)
    cross(1)
    finish(1)
    for copy in started:
        copy.wait_send()


def thresholds(near_mask, far_pattern, window, frame_id):
    blocks = jnp.arange(128, dtype=jnp.int32)
    slab = blocks // 2
    away = jnp.abs(slab - frame_id)
    limit = jnp.sum(
        jnp.where(
            jnp.arange(32, dtype=jnp.int32)[:, None] == away[None, :], window[:, None], 0
        ),
        axis=0,
    )
    far = jnp.pad(far_pattern, ((0, 0), (0, 64)))
    first = jnp.where(slab < frame_id, 0, 2)
    odd = blocks % 2
    near = jnp.where(
        first[None, :] == 0,
        jnp.where(odd[None, :] == 0, near_mask[:, 0:1], near_mask[:, 1:2]),
        jnp.where(odd[None, :] == 0, near_mask[:, 2:3], near_mask[:, 3:4]),
    )
    chosen = jnp.where(away[None, :] == 0, 1, jnp.where(away[None, :] == 1, near, far))
    table = jnp.where(chosen > 0, limit[None, :], 0).astype(F32)
    return jnp.pad(table, ((0, 6), (0, 0)))


def per_device(tokens, w_qkv, norm_gains, w_out, near_mask, far_pattern, window):
    table = thresholds(near_mask, far_pattern, window, lax.axis_index("frame"))
    any_spec = pl.BlockSpec(memory_space=pl.ANY)
    vmem_spec = pl.BlockSpec(memory_space=pltpu.VMEM)
    dma = pltpu.SemaphoreType.DMA
    out, checks = pl.pallas_call(
        layer_kernel,
        name="layer",
        out_shape=(
            jax.ShapeDtypeStruct((SLAB, COLS), BF),
            jax.ShapeDtypeStruct((2, 8, BLK), F32),
        ),
        in_specs=[any_spec, any_spec, any_spec, vmem_spec, vmem_spec],
        out_specs=(vmem_spec, vmem_spec),
        scratch_shapes=[
            pltpu.VMEM((SLAB, D), BF),
            pltpu.VMEM((HL, D, 2 * HD), BF),
            pltpu.VMEM((D, COLS), BF),
            pltpu.VMEM((COLS, D), BF),
            pltpu.VMEM((HL, 8, SLAB, 2 * HD), BF),
            pltpu.VMEM((HL, 4, SLAB, HD), BF),
            pltpu.VMEM((4, 8, 128), F32),
            pltpu.VMEM((8, 32, SLAB), F32),
            pltpu.VMEM((2, BLK, SLAB), F32),
            pltpu.VMEM((4 * BLK, 8 * SLAB), BF),
            pltpu.VMEM((6, BLK, HD), F32),
            pltpu.VMEM((6, BLK, HD), F32),
            pltpu.VMEM((6, 3, OROWS, HD), BF),
            pltpu.VMEM((6, CUT, HD), BF),
            pltpu.VMEM((6, OROWS - CUT, HD), BF),
            pltpu.VMEM((6, 2, OROWS, HD), BF),
            pltpu.VMEM((2, 4, BLK, COLS), F32),
            pltpu.VMEM((2, 2, BLK, COLS), BF),
            pltpu.VMEM((2, 2, BLK, COLS), BF),
            pltpu.VMEM((2, 2, 2, BLK, COLS), BF),
            pltpu.VMEM((2, 2, 2, BLK, COLS), BF),
            pltpu.VMEM((2, BLK, COLS), BF),
            pltpu.VMEM((2, BLK, COLS), BF),
            pltpu.VMEM((2, 8, 8, BLK), F32),
            dma((9,)),
            dma((HL, 8)),
            dma((HL, 8)),
            dma((HL, 4)),
            dma((HL, 4)),
            dma((3,)),
            dma((3,)),
            dma((6, 6)),
            dma((6, 6)),
            dma((2, 7)),
            dma((2, 7)),
            dma((2, 8)),
            dma((2, 8)),
        ],
        compiler_params=pltpu.CompilerParams(
            collective_id=0, has_side_effects=True, vmem_limit_bytes=56 * 1024 * 1024
        ),
    )(tokens, w_qkv, w_out, norm_gains, table)
    return out, checks[:, 0, :].reshape(SLAB)


def solution(mesh):
    in_specs = (
        P("frame", None),
        P(None, None, "head"),
        P(None, "head"),
        P("head", None),
        P("frame", None),
        P("frame", None),
        P(),
    )
    out_specs = (P("frame", "head"), P("frame"))
    return jax.shard_map(
        per_device, mesh=mesh, in_specs=in_specs, out_specs=out_specs, check_vma=False
    )
```

```python
import jax
import jax.numpy as jnp
from jax import lax
from jax.experimental import pallas as pl
from jax.experimental.pallas import tpu as pltpu
from jax.sharding import PartitionSpec as P

D = 3072
HD = 128
BLK = 128
SLAB = 256
HL = 3
COLS = HL * HD
POOL = 40
PART = 1024
MESH = pl.DeviceIdType.MESH
BF = jnp.bfloat16
F32 = jnp.float32
LOG2E = 1.4426950408889634
OROWS = BLK + 8
NT = (((1,), (1,)), ((), ()))


def layer_kernel(
    tok_hbm,
    w_hbm,
    wo_hbm,
    gains_hbm,
    near_hbm,
    far_hbm,
    window_hbm,
    out_ref,
    cs_ref,
    tok,
    wkv,
    wq,
    wx,
    kv,
    qb,
    gains_ref,
    near_ref,
    far_ref,
    window_ref,
    far,
    tbuf,
    texp,
    dist,
    pbuf,
    acc,
    num,
    tot,
    osend,
    orel,
    ofin,
    ab,
    po,
    zs,
    zr,
    csb,
    lsem,
    pool,
    krs,
    qrs,
    trs,
    wrs,
    ors,
    ars,
    zrs,
    crs,
):
    f = lax.axis_index("frame")
    g = lax.axis_index("head")
    zh, y, c = f // 8, (f // 2) % 4, f % 2
    zl, x = g // 4, g % 4

    def at_y(step):
        return (zh * 8 + ((y + step) % 4) * 2 + c, g)

    def at_z(step):
        return (((zh + step) % 4) * 8 + y * 2 + c, g)

    def at_x(step):
        return (f, zl * 4 + (x + step) % 4)

    core = (zh * 8 + y * 2 + (1 - c), g)
    zlo = (f, (1 - zl) * 4 + x)

    started = []
    waited = set()

    def sent(i):
        if i not in waited:
            waited.add(i)
            started[i].wait_send()

    def send(src, dst, rsem, dev):
        n = len(started)
        if n >= POOL:
            sent(n - POOL)
        copy = pltpu.make_async_remote_copy(
            src_ref=src,
            dst_ref=dst,
            send_sem=pool.at[n % POOL],
            recv_sem=rsem,
            device_id=dev,
            device_id_type=MESH,
        )
        copy.start()
        started.append(copy)
        return copy

    def fetch(src, dst, i):
        copy = pltpu.make_async_copy(src, dst, lsem.at[i])
        copy.start()
        return copy

    def columns(side, step):
        at = (side * 4 + (x + step) % 4) * COLS
        return pl.ds(pl.multiple_of(at, HD), COLS)

    barrier = pltpu.get_barrier_semaphore()
    peers = [at_y(1), at_y(3), core, at_z(1), at_z(3)]
    peers += [(f, (g + k) % 8) for k in range(1, 8)]
    for peer in peers:
        pl.semaphore_signal(barrier, inc=1, device_id=peer, device_id_type=MESH)

    small_in = [
        fetch(near_hbm, near_ref, 10),
        fetch(window_hbm, window_ref, 11),
        fetch(far_hbm, far_ref, 12),
        fetch(gains_hbm, gains_ref, 13),
    ]
    q_in = []
    for k in range(3):
        span = pl.ds(k * PART, PART)
        tok_at = fetch(tok_hbm.at[:, span], tok.at[:, span], (0, 14, 15)[k])
        q_in.append((tok_at, fetch(w_hbm.at[0, span], wq.at[span], (7, 16, 17)[k])))
    kv_in = []
    for h in range(HL):
        hs = pl.ds(h * HD, HD)
        kv_in.append(
            (
                fetch(w_hbm.at[1, :, hs], wkv.at[h, :, pl.ds(0, HD)], 1 + 2 * h),
                fetch(w_hbm.at[2, :, hs], wkv.at[h, :, pl.ds(HD, HD)], 2 + 2 * h),
            )
        )
    wx_in = (
        fetch(wo_hbm.at[:, columns(c, 0)], wx.at[0, 0], 8),
        fetch(wo_hbm.at[:, columns(1 - c, 0)], wx.at[0, 1], 9),
    )

    for copy in small_in:
        copy.wait()
    lane = lax.broadcasted_iota(jnp.int32, (8, 128), 1)
    line = lax.broadcasted_iota(jnp.int32, (8, 128), 0)
    slabs = lax.shift_right_logical(lane, 1)
    odd = lane - 2 * slabs
    apart = jnp.abs(slabs - f)
    limits = jnp.zeros((8, 128), jnp.int32)
    for d in range(32):
        limits = jnp.where(apart == d, window_ref[d], limits)
    near = []
    for a in range(2):
        before = jnp.where(odd == 1, near_ref[a, 1], near_ref[a, 0])
        after = jnp.where(odd == 1, near_ref[a, 3], near_ref[a, 2])
        near.append(jnp.where(slabs < f, before, after))
    far[...] = jnp.zeros((8, 128), jnp.int32)
    far[0:2, 0:64] = far_ref[...]
    chosen = jnp.where(apart == 1, jnp.where(line == 0, near[0], near[1]), far[...])
    chosen = jnp.where(apart == 0, 1, chosen)
    tbuf[0] = jnp.where(chosen > 0, limits, 0).astype(F32)

    def make_kv(h):
        for copy in kv_in[h]:
            copy.wait()
        both = jnp.dot(tok[...], wkv[h], preferred_element_type=F32)
        key = both[:, :HD]
        factor = lax.rsqrt(jnp.mean(key * key, axis=1, keepdims=True) + 1e-06)
        gain = gains_ref[1:2, h * HD : (h + 1) * HD]
        kv[h, 0, :, 0:HD] = (key * factor * gain).astype(BF)
        kv[h, 0, :, HD : 2 * HD] = both[:, HD:].astype(BF)

    def make_q():
        whole = None
        for k in range(3):
            for copy in q_in[k]:
                copy.wait()
            span = slice(k * PART, (k + 1) * PART)
            part = jnp.dot(tok[:, span], wq[span, :], preferred_element_type=F32)
            whole = part if whole is None else whole + part
        for h in range(HL):
            query = whole[:, h * HD : (h + 1) * HD]
            factor = lax.rsqrt(jnp.mean(query * query, axis=1, keepdims=True) + 1e-06)
            gain = gains_ref[0:1, h * HD : (h + 1) * HD] * (HD**-0.5 * LOG2E)
            qb[h, 0] = (query * factor * gain).astype(BF)

    top, low = pl.ds(0, BLK), pl.ds(BLK, BLK)
    kcopy, qcopy, tcopy, wcopy, ocopy, acopy = {}, {}, {}, {}, {}, {}

    def send_kv(h):
        own = kv.at[h, 0]
        kcopy[h, "R"] = send(own, kv.at[h, 1], krs.at[h, 0], at_y(1))
        kcopy[h, "L"] = send(own, kv.at[h, 2], krs.at[h, 1], at_y(3))
        kcopy[h, "c0"] = send(own, kv.at[h, 4], krs.at[h, 2], core)

    def relay_kv(h):
        kcopy[h, "R"].wait_recv()
        kcopy[h, "RR"] = send(
            kv.at[h, 1, top], kv.at[h, 3, top], krs.at[h, 3], at_y(1)
        )
        kcopy[h, "c1"] = send(kv.at[h, 1], kv.at[h, 5], krs.at[h, 4], core)
        kcopy[h, "L"].wait_recv()
        kcopy[h, "LL"] = send(
            kv.at[h, 2, low], kv.at[h, 3, low], krs.at[h, 5], at_y(3)
        )
        kcopy[h, "c2"] = send(kv.at[h, 2], kv.at[h, 6], krs.at[h, 6], core)

    def last_kv(h):
        kcopy[h, "RR"].wait_recv()
        kcopy[h, "LL"].wait_recv()
        kcopy[h, "c3"] = send(kv.at[h, 3], kv.at[h, 7], krs.at[h, 7], core)

    def arrived_kv(h):
        for name in ("c0", "c1", "c2", "c3"):
            kcopy[h, name].wait_recv()

    def send_ring(buf, copies, rsem, to, h):
        own = buf.at[h, 0]
        copies[h, "R"] = send(own, buf.at[h, 1], rsem.at[h, 0], to(1))
        copies[h, "L"] = send(own, buf.at[h, 2], rsem.at[h, 1], to(3))

    def relay_ring(buf, copies, rsem, to, h):
        copies[h, "R"].wait_recv()
        copies[h, "RR"] = send(
            buf.at[h, 1, top], buf.at[h, 3, top], rsem.at[h, 2], to(1)
        )
        copies[h, "L"].wait_recv()
        copies[h, "LL"] = send(
            buf.at[h, 2, low], buf.at[h, 3, low], rsem.at[h, 3], to(3)
        )

    def arrived_ring(copies, h):
        copies[h, "RR"].wait_recv()
        copies[h, "LL"].wait_recv()

    def send_q(h):
        send_ring(qb, qcopy, qrs, at_z, h)

    def relay_q(h):
        relay_ring(qb, qcopy, qrs, at_z, h)

    def arrived_q(h):
        arrived_ring(qcopy, h)

    def send_t():
        tcopy["R"] = send(tbuf.at[0], tbuf.at[1], trs.at[0], at_z(1))
        tcopy["L"] = send(tbuf.at[0], tbuf.at[2], trs.at[1], at_z(3))

    def relay_t():
        tcopy["R"].wait_recv()
        tcopy["RR"] = send(tbuf.at[1], tbuf.at[3], trs.at[2], at_z(1))
        tcopy["L"].wait_recv()

    def send_w():
        for k, step in ((1, 1), (2, 3), (3, 2)):
            wcopy[k] = send(
                wo_hbm.at[:, columns(c, step)], wx.at[k, 0], wrs.at[k], at_x(step)
            )

    def share_w():
        for k in (1, 2, 3):
            wcopy[k].wait_recv()
            wcopy[k + 3] = send(wx.at[k, 0], wx.at[k, 1], wrs.at[k + 3], core)

    def arrived_w():
        for copy in wx_in:
            copy.wait()
        for k in (4, 5, 6):
            wcopy[k].wait_recv()

    def limits_table():
        row = lax.broadcasted_iota(jnp.int32, (BLK, SLAB), 0)
        col = lax.broadcasted_iota(jnp.int32, (BLK, SLAB), 1)
        for rh in range(2):
            dist[rh] = jnp.abs(row + rh * BLK - col).astype(F32)
        tcopy["RR"].wait_recv()
        table = tbuf[...].reshape(4 * 8, 128).astype(BF)
        half = (col >= BLK).astype(jnp.int32)
        for j in range(8):
            slab = zh * 8 + ((y + (0, 3, 1, 2)[j % 4]) % 4) * 2 + (c if j < 4 else 1 - c)
            pick = (row == half + slab * 2).astype(F32).astype(BF)
            texp[j] = jnp.dot(table, pick, preferred_element_type=F32)

    def attend(h, slots):
        size = SLAB * len(slots)
        queries = jnp.concatenate([qb[h, q] for q in slots], axis=0)

        for k in range(4):
            pair = slice(2 * k, 2 * k + 2)
            cols = slice(2 * k * SLAB, (2 * k + 2) * SLAB)
            for j in range(2 * k, 2 * k + 2):
                raw = lax.dot_general(queries, kv[h, j, :, 0:HD], NT, preferred_element_type=F32)
                for i, q in enumerate(slots):
                    for rh in range(2):
                        rows = slice(i * SLAB + rh * BLK, i * SLAB + (rh + 1) * BLK)
                        limit = texp[j, q * 8 + rh : q * 8 + rh + 1, :]
                        weight = jnp.where(dist[rh] < limit, jnp.exp2(raw[rows]), 0.0)
                        pbuf[rows, j * SLAB : (j + 1) * SLAB] = weight.astype(BF)
            values = kv[h, pair, :, HD : 2 * HD].reshape(2 * SLAB, HD)
            values = jnp.concatenate([values, jnp.ones((2 * SLAB, HD), BF)], axis=1)
            part = jnp.dot(pbuf[0:size, cols], values, preferred_element_type=F32)
            if k == 0:
                acc[0:size, :] = part
            else:
                acc[0:size, :] += part
        return acc[0:size, :]

    def pack(h, dest, part):
        for half in range(2):
            rows = part[half * BLK : (half + 1) * BLK]
            osend[h, dest, half, 0:BLK, :] = rows[:, :HD].astype(BF)
            osend[h, dest, half, BLK:OROWS, :] = rows[:, HD:].T[0:8].astype(BF)

    def attend_opp(h):
        pack(h, 2, attend(h, (3,)))
        ocopy[h, "RR"] = send(
            osend.at[h, 2, 0], orel.at[h, 0], ors.at[h, 0], at_z(1)
        )
        ocopy[h, "LL"] = send(
            osend.at[h, 2, 1], orel.at[h, 1], ors.at[h, 1], at_z(3)
        )

    def attend_sides(h):
        result = attend(h, (1, 2))
        pack(h, 0, result[:SLAB])
        pack(h, 1, result[SLAB:])
        ocopy[h, "R1"] = send(
            osend.at[h, 1, 1], ofin.at[h, 0, 1], ors.at[h, 2], at_z(1)
        )
        ocopy[h, "L0"] = send(
            osend.at[h, 0, 0], ofin.at[h, 1, 0], ors.at[h, 3], at_z(3)
        )

    def relay_o(h):
        ocopy[h, "RR"].wait_recv()
        osend[h, 1, 0] = (osend[h, 1, 0].astype(F32) + orel[h, 0].astype(F32)).astype(BF)
        ocopy[h, "R0"] = send(
            osend.at[h, 1, 0], ofin.at[h, 0, 0], ors.at[h, 4], at_z(1)
        )
        ocopy[h, "LL"].wait_recv()
        osend[h, 0, 1] = (osend[h, 0, 1].astype(F32) + orel[h, 1].astype(F32)).astype(BF)
        ocopy[h, "L1"] = send(
            osend.at[h, 0, 1], ofin.at[h, 1, 1], ors.at[h, 5], at_z(3)
        )

    def attend_own(h):
        result = attend(h, (0,))
        num[h] = result[:, :HD]
        tot[h] = result[:, HD:]

    def combine(h):
        for name in ("R0", "R1", "L0", "L1"):
            ocopy[h, name].wait_recv()
        for half in range(2):
            more = ofin[h, 0, half].astype(F32) + ofin[h, 1, half].astype(F32)
            rows = slice(half * BLK, (half + 1) * BLK)
            strip = more[BLK:OROWS]
            total = tot[h, rows, :] + jnp.concatenate([strip] * 16, axis=0).T
            ab[h, 0, rows, :] = ((num[h, rows, :] + more[:BLK]) / total).astype(BF)
        send_ring(ab, acopy, ars, at_x, h)

    def relay_a(h):
        relay_ring(ab, acopy, ars, at_x, h)

    def arrived_a(h):
        arrived_ring(acopy, h)

    def last_rows(pair, side):
        rows = jnp.concatenate([ab[2, pair], ab[2, pair + 1]], axis=1)
        block = jnp.concatenate(
            [wx[pair, side, 2 * HD : COLS, :], wx[pair + 1, side, 2 * HD : COLS, :]], axis=0
        )
        return jnp.dot(rows, block, preferred_element_type=F32)

    def project_first():
        for side in range(2):
            total = None
            for k in range(4):
                rows = jnp.concatenate([ab[0, k], ab[1, k]], axis=1)
                part = jnp.dot(rows, wx[k, side, 0 : 2 * HD, :], preferred_element_type=F32)
                total = part if total is None else total + part
            po[side] = total

    def project_near():
        for side in range(2):
            po[side] = po[side] + last_rows(0, side)

    def finish():
        other = (c + zl + 1) % 2
        given = po[other] + last_rows(2, other)
        zs[...] = given.astype(BF)
        zcopy = send(zs, zr, zrs.at[0], zlo)
        kept = po[1 - other] + last_rows(2, 1 - other)
        sums = given + kept
        turned = (sums[:, :HD] + sums[:, HD : 2 * HD] + sums[:, 2 * HD :]).T
        total = jnp.sum(turned, axis=0, keepdims=True) * D ** (-0.5)
        csb[g] = jnp.broadcast_to(total, (8, SLAB))
        for k in range(1, 8):
            send(csb.at[g], csb.at[g], crs.at[k], (f, (g + k) % 8))
        po[0] = kept
        for k in range(1, 8):
            pltpu.make_async_remote_copy(
                src_ref=csb.at[(g + 8 - k) % 8],
                dst_ref=csb.at[(g + 8 - k) % 8],
                send_sem=pool.at[0],
                recv_sem=crs.at[k],
                device_id=(f, (g + k) % 8),
                device_id_type=MESH,
            ).wait_recv()
        checks = csb[0]
        for k in range(1, 8):
            checks = checks + csb[k]
        cs_ref[...] = checks[0]
        zcopy.wait_recv()
        out_ref[...] = (po[0] + zr[...].astype(F32)).astype(BF)

    def drain():
        for i in range(len(started)):
            sent(i)

    make_q()
    pl.semaphore_wait(barrier, len(peers))
    send_t()
    send_q(0)
    send_q(1)
    send_q(2)
    make_kv(0)
    send_kv(0)
    make_kv(1)
    send_kv(1)
    make_kv(2)
    send_kv(2)
    send_w()
    relay_t()
    relay_q(0)
    relay_kv(0)
    relay_q(1)
    relay_kv(1)
    relay_q(2)
    relay_kv(2)
    last_kv(0)
    limits_table()
    arrived_q(0)
    arrived_kv(0)
    attend_opp(0)
    last_kv(1)
    attend_sides(0)
    last_kv(2)
    arrived_kv(1)
    arrived_q(1)
    attend_opp(1)
    arrived_kv(2)
    arrived_q(2)
    attend_opp(2)
    attend_sides(1)
    relay_o(0)
    attend_sides(2)
    share_w()
    attend_own(0)
    relay_o(1)
    attend_own(1)
    attend_own(2)
    relay_o(2)
    combine(0)
    combine(1)
    arrived_w()
    relay_a(0)
    combine(2)
    relay_a(1)
    drain()
    relay_a(2)
    arrived_a(0)
    arrived_a(1)
    project_first()
    project_near()
    arrived_a(2)
    finish()
    drain()


def per_device(tokens, w_qkv, norm_gains, w_out, near_mask, far_pattern, window):
    any_spec = pl.BlockSpec(memory_space=pl.ANY)
    vmem_spec = pl.BlockSpec(memory_space=pltpu.VMEM)
    dma = pltpu.SemaphoreType.DMA
    return pl.pallas_call(
        layer_kernel,
        name="layer",
        out_shape=(
            pltpu.VMEM((SLAB, COLS), BF),
            pltpu.VMEM((SLAB,), F32),
        ),
        in_specs=[any_spec] * 7,
        out_specs=(vmem_spec, vmem_spec),
        scratch_shapes=[
            pltpu.VMEM((SLAB, D), BF),
            pltpu.VMEM((HL, D, 2 * HD), BF),
            pltpu.VMEM((D, COLS), BF),
            pltpu.VMEM((4, 2, COLS, COLS), BF),
            pltpu.VMEM((HL, 8, SLAB, 2 * HD), BF),
            pltpu.VMEM((HL, 4, SLAB, HD), BF),
            pltpu.VMEM((2, COLS), F32),
            pltpu.SMEM((2, 4), jnp.int32),
            pltpu.VMEM((2, 64), jnp.int32),
            pltpu.SMEM((32,), jnp.int32),
            pltpu.VMEM((8, 128), jnp.int32),
            pltpu.VMEM((4, 8, 128), F32),
            pltpu.VMEM((8, 32, SLAB), F32),
            pltpu.VMEM((2, BLK, SLAB), F32),
            pltpu.VMEM((2 * SLAB, 8 * SLAB), BF),
            pltpu.VMEM((2 * SLAB, 2 * HD), F32),
            pltpu.VMEM((HL, SLAB, HD), F32),
            pltpu.VMEM((HL, SLAB, HD), F32),
            pltpu.VMEM((HL, 3, 2, OROWS, HD), BF),
            pltpu.VMEM((HL, 2, OROWS, HD), BF),
            pltpu.VMEM((HL, 2, 2, OROWS, HD), BF),
            pltpu.VMEM((HL, 4, SLAB, HD), BF),
            pltpu.VMEM((2, SLAB, COLS), F32),
            pltpu.VMEM((SLAB, COLS), BF),
            pltpu.VMEM((SLAB, COLS), BF),
            pltpu.VMEM((8, 8, SLAB), F32),
            dma((14 + 4,)),
            dma((POOL,)),
            dma((HL, 8)),
            dma((HL, 4)),
            dma((3,)),
            dma((7,)),
            dma((HL, 6)),
            dma((HL, 4)),
            dma((1,)),
            dma((8,)),
        ],
        compiler_params=pltpu.CompilerParams(
            collective_id=0, has_side_effects=True, vmem_limit_bytes=56 * 1024 * 1024
        ),
    )(tokens, w_qkv, w_out, norm_gains, near_mask, far_pattern, window)


def solution(mesh):
    in_specs = (
        P("frame", None),
        P(None, None, "head"),
        P(None, "head"),
        P("head", None),
        P("frame", None),
        P("frame", None),
        P(),
    )
    out_specs = (P("frame", "head"), P("frame"))
    return jax.shard_map(
        per_device, mesh=mesh, in_specs=in_specs, out_specs=out_specs, check_vma=False
    )
```

```python
import jax
import jax.numpy as jnp
from jax import lax
from jax.experimental import pallas as pl
from jax.experimental.pallas import tpu as pltpu
from jax.sharding import PartitionSpec as P

D = 3072
HD = 128
BLK = 128
SLAB = 256
HL = 3
COLS = HL * HD
POOL = 40
PART = 1024
MESH = pl.DeviceIdType.MESH
BF = jnp.bfloat16
F32 = jnp.float32
LOG2E = 1.4426950408889634
OROWS = BLK + 8
NT = (((1,), (1,)), ((), ()))


def layer_kernel(
    tok_hbm,
    w_hbm,
    wo_hbm,
    gains_hbm,
    near_hbm,
    far_hbm,
    window_hbm,
    out_ref,
    cs_ref,
    tok,
    wkv,
    wq,
    wx,
    kv,
    qb,
    gains_ref,
    near_ref,
    far_ref,
    window_ref,
    far,
    tbuf,
    texp,
    dist,
    pbuf,
    acc,
    num,
    tot,
    osend,
    orel,
    ofin,
    ab,
    po,
    zs,
    zr,
    csb,
    pool,
    krs,
    qrs,
    trs,
    wrs,
    ors,
    ars,
    zrs,
    crs,
):
    f = lax.axis_index("frame")
    g = lax.axis_index("head")
    zh, y, c = f // 8, (f // 2) % 4, f % 2
    zl, x = g // 4, g % 4

    def at_y(step):
        return (zh * 8 + ((y + step) % 4) * 2 + c, g)

    def at_z(step):
        return (((zh + step) % 4) * 8 + y * 2 + c, g)

    def at_x(step):
        return (f, zl * 4 + (x + step) % 4)

    core = (zh * 8 + y * 2 + (1 - c), g)
    zlo = (f, (1 - zl) * 4 + x)

    started = []
    waited = set()

    def sent(i):
        if i not in waited:
            waited.add(i)
            started[i].wait_send()

    def send(src, dst, rsem, dev):
        n = len(started)
        if n >= POOL:
            sent(n - POOL)
        copy = pltpu.make_async_remote_copy(
            src_ref=src,
            dst_ref=dst,
            send_sem=pool.at[n % POOL],
            recv_sem=rsem,
            device_id=dev,
            device_id_type=MESH,
        )
        copy.start()
        started.append(copy)
        return copy

    def fetch(src, dst, i):
        copy = pltpu.make_async_copy(src, dst, pool.at[POOL - 21 + i])
        copy.start()
        return copy

    def columns(side, step):
        at = (side * 4 + (x + step) % 4) * COLS
        return pl.ds(pl.multiple_of(at, HD), COLS)

    barrier = pltpu.get_barrier_semaphore()
    peers = [at_y(1), at_y(3), core, at_z(1), at_z(3)]
    peers += [(f, (g + k) % 8) for k in range(1, 8)]
    for peer in peers:
        pl.semaphore_signal(barrier, inc=1, device_id=peer, device_id_type=MESH)

    small_in = [
        fetch(near_hbm, near_ref, 10),
        fetch(window_hbm, window_ref, 11),
        fetch(far_hbm, far_ref, 12),
        fetch(gains_hbm, gains_ref, 13),
    ]
    kv_in = []
    for k in range(3):
        span = pl.ds(k * PART, PART)
        kv_in.append(
            (
                fetch(tok_hbm.at[:, span], tok.at[:, span], 3 * k),
                fetch(w_hbm.at[1, span, pl.ds(0, HD)], wkv.at[0, span, pl.ds(0, HD)], 3 * k + 1),
                fetch(w_hbm.at[2, span, pl.ds(0, HD)], wkv.at[0, span, pl.ds(HD, HD)], 3 * k + 2),
            )
        )
    first, rest = pl.ds(0, HD), pl.ds(HD, 2 * HD)
    q_first = fetch(w_hbm.at[0, :, first], wq.at[:, first], 14)
    q_rest = fetch(w_hbm.at[0, :, rest], wq.at[:, rest], 15)
    later_in = {}
    for h in (1, 2):
        hs = pl.ds(h * HD, HD)
        later_in[h] = (
            fetch(w_hbm.at[1, :, hs], wkv.at[h, :, pl.ds(0, HD)], 14 + 2 * h),
            fetch(w_hbm.at[2, :, hs], wkv.at[h, :, pl.ds(HD, HD)], 15 + 2 * h),
        )
    wx_in = (
        fetch(wo_hbm.at[:, columns(c, 0)], wx.at[0, 0], 9),
        fetch(wo_hbm.at[:, columns(1 - c, 0)], wx.at[0, 1], 20),
    )

    for copy in small_in:
        copy.wait()
    lane = lax.broadcasted_iota(jnp.int32, (8, 128), 1)
    line = lax.broadcasted_iota(jnp.int32, (8, 128), 0)
    slabs = lax.shift_right_logical(lane, 1)
    odd = lane - 2 * slabs
    apart = jnp.abs(slabs - f)
    limits = jnp.zeros((8, 128), jnp.int32)
    for d in range(32):
        limits = jnp.where(apart == d, window_ref[d], limits)
    near = []
    for a in range(2):
        before = jnp.where(odd == 1, near_ref[a, 1], near_ref[a, 0])
        after = jnp.where(odd == 1, near_ref[a, 3], near_ref[a, 2])
        near.append(jnp.where(slabs < f, before, after))
    far[...] = jnp.zeros((8, 128), jnp.int32)
    far[0:2, 0:64] = far_ref[...]
    chosen = jnp.where(apart == 1, jnp.where(line == 0, near[0], near[1]), far[...])
    chosen = jnp.where(apart == 0, 1, chosen)
    tbuf[0] = jnp.where(chosen > 0, limits, 0).astype(F32)

    def keep_kv(h, both):
        key = both[:, :HD]
        factor = lax.rsqrt(jnp.mean(key * key, axis=1, keepdims=True) + 1e-06)
        gain = gains_ref[1:2, h * HD : (h + 1) * HD]
        kv[h, 0, :, 0:HD] = (key * factor * gain).astype(BF)
        kv[h, 0, :, HD : 2 * HD] = both[:, HD:].astype(BF)

    def make_first():
        both = None
        for k in range(3):
            for copy in kv_in[k]:
                copy.wait()
            span = slice(k * PART, (k + 1) * PART)
            part = jnp.dot(tok[:, span], wkv[0, span, :], preferred_element_type=F32)
            both = part if both is None else both + part
        keep_kv(0, both)

    def make_kv(h):
        for copy in later_in[h]:
            copy.wait()
        keep_kv(h, jnp.dot(tok[...], wkv[h], preferred_element_type=F32))

    def keep_q(h, query):
        factor = lax.rsqrt(jnp.mean(query * query, axis=1, keepdims=True) + 1e-06)
        gain = gains_ref[0:1, h * HD : (h + 1) * HD] * (HD**-0.5 * LOG2E)
        qb[h, 0] = (query * factor * gain).astype(BF)

    def make_q():
        q_first.wait()
        keep_q(0, jnp.dot(tok[...], wq[:, 0:HD], preferred_element_type=F32))

    def make_rest():
        q_rest.wait()
        both = jnp.dot(tok[...], wq[:, HD:], preferred_element_type=F32)
        keep_q(1, both[:, :HD])
        keep_q(2, both[:, HD:])

    top, low = pl.ds(0, BLK), pl.ds(BLK, BLK)
    kcopy, qcopy, tcopy, wcopy, ocopy, acopy = {}, {}, {}, {}, {}, {}

    def send_kv(h):
        own = kv.at[h, 0]
        kcopy[h, "R"] = send(own, kv.at[h, 1], krs.at[h, 0], at_y(1))
        kcopy[h, "L"] = send(own, kv.at[h, 2], krs.at[h, 1], at_y(3))
        kcopy[h, "c0"] = send(own, kv.at[h, 4], krs.at[h, 2], core)

    def relay_kv(h):
        kcopy[h, "R"].wait_recv()
        kcopy[h, "RR"] = send(
            kv.at[h, 1, top], kv.at[h, 3, top], krs.at[h, 3], at_y(1)
        )
        kcopy[h, "c1"] = send(kv.at[h, 1], kv.at[h, 5], krs.at[h, 4], core)
        kcopy[h, "L"].wait_recv()
        kcopy[h, "LL"] = send(
            kv.at[h, 2, low], kv.at[h, 3, low], krs.at[h, 5], at_y(3)
        )
        kcopy[h, "c2"] = send(kv.at[h, 2], kv.at[h, 6], krs.at[h, 6], core)

    def last_kv(h):
        kcopy[h, "RR"].wait_recv()
        kcopy[h, "LL"].wait_recv()
        kcopy[h, "c3"] = send(kv.at[h, 3], kv.at[h, 7], krs.at[h, 7], core)

    def arrived_kv(h):
        for name in ("c0", "c1", "c2", "c3"):
            kcopy[h, name].wait_recv()

    def send_ring(buf, copies, rsem, to, h):
        own = buf.at[h, 0]
        copies[h, "R"] = send(own, buf.at[h, 1], rsem.at[h, 0], to(1))
        copies[h, "L"] = send(own, buf.at[h, 2], rsem.at[h, 1], to(3))

    def relay_ring(buf, copies, rsem, to, h):
        copies[h, "R"].wait_recv()
        copies[h, "RR"] = send(
            buf.at[h, 1, top], buf.at[h, 3, top], rsem.at[h, 2], to(1)
        )
        copies[h, "L"].wait_recv()
        copies[h, "LL"] = send(
            buf.at[h, 2, low], buf.at[h, 3, low], rsem.at[h, 3], to(3)
        )

    def arrived_ring(copies, h):
        copies[h, "RR"].wait_recv()
        copies[h, "LL"].wait_recv()

    def send_q(h):
        send_ring(qb, qcopy, qrs, at_z, h)

    def relay_q(h):
        relay_ring(qb, qcopy, qrs, at_z, h)

    def arrived_q(h):
        arrived_ring(qcopy, h)

    def send_t():
        tcopy["R"] = send(tbuf.at[0], tbuf.at[1], trs.at[0], at_z(1))
        tcopy["L"] = send(tbuf.at[0], tbuf.at[2], trs.at[1], at_z(3))

    def relay_t():
        tcopy["R"].wait_recv()
        tcopy["RR"] = send(tbuf.at[1], tbuf.at[3], trs.at[2], at_z(1))
        tcopy["L"].wait_recv()

    def send_w():
        for k, step in ((1, 1), (2, 3), (3, 2)):
            wcopy[k] = send(
                wo_hbm.at[:, columns(c, step)], wx.at[k, 0], wrs.at[k], at_x(step)
            )

    def share_w():
        for k in (1, 2, 3):
            wcopy[k].wait_recv()
            wcopy[k + 3] = send(wx.at[k, 0], wx.at[k, 1], wrs.at[k + 3], core)

    def arrived_w():
        for k in (4, 5, 6):
            wcopy[k].wait_recv()

    def limits_table():
        row = lax.broadcasted_iota(jnp.int32, (BLK, SLAB), 0)
        col = lax.broadcasted_iota(jnp.int32, (BLK, SLAB), 1)
        for rh in range(2):
            dist[rh] = jnp.abs(row + rh * BLK - col).astype(F32)
        tcopy["RR"].wait_recv()
        table = tbuf[...].reshape(4 * 8, 128).astype(BF)
        half = (col >= BLK).astype(jnp.int32)
        for j in range(8):
            slab = zh * 8 + ((y + (0, 3, 1, 2)[j % 4]) % 4) * 2 + (c if j < 4 else 1 - c)
            pick = (row == half + slab * 2).astype(F32).astype(BF)
            texp[j] = jnp.dot(table, pick, preferred_element_type=F32)

    def attend(h, slots):
        size = SLAB * len(slots)
        queries = jnp.concatenate([qb[h, q] for q in slots], axis=0)

        for k in range(4):
            pair = slice(2 * k, 2 * k + 2)
            cols = slice(2 * k * SLAB, (2 * k + 2) * SLAB)
            for j in range(2 * k, 2 * k + 2):
                raw = lax.dot_general(queries, kv[h, j, :, 0:HD], NT, preferred_element_type=F32)
                for i, q in enumerate(slots):
                    for rh in range(2):
                        rows = slice(i * SLAB + rh * BLK, i * SLAB + (rh + 1) * BLK)
                        limit = texp[j, q * 8 + rh : q * 8 + rh + 1, :]
                        weight = jnp.where(dist[rh] < limit, jnp.exp2(raw[rows]), 0.0)
                        pbuf[rows, j * SLAB : (j + 1) * SLAB] = weight.astype(BF)
            values = kv[h, pair, :, HD : 2 * HD].reshape(2 * SLAB, HD)
            values = jnp.concatenate([values, jnp.ones((2 * SLAB, HD), BF)], axis=1)
            part = jnp.dot(pbuf[0:size, cols], values, preferred_element_type=F32)
            if k == 0:
                acc[0:size, :] = part
            else:
                acc[0:size, :] += part
        return acc[0:size, :]

    def pack(h, dest, part):
        for half in range(2):
            rows = part[half * BLK : (half + 1) * BLK]
            osend[h, dest, half, 0:BLK, :] = rows[:, :HD].astype(BF)
            osend[h, dest, half, BLK:OROWS, :] = rows[:, HD:].T[0:8].astype(BF)

    def attend_opp(h):
        pack(h, 2, attend(h, (3,)))
        ocopy[h, "RR"] = send(
            osend.at[h, 2, 0], orel.at[h, 0], ors.at[h, 0], at_z(1)
        )
        ocopy[h, "LL"] = send(
            osend.at[h, 2, 1], orel.at[h, 1], ors.at[h, 1], at_z(3)
        )

    def attend_sides(h):
        result = attend(h, (1, 2))
        pack(h, 0, result[:SLAB])
        pack(h, 1, result[SLAB:])
        ocopy[h, "R1"] = send(
            osend.at[h, 1, 1], ofin.at[h, 0, 1], ors.at[h, 2], at_z(1)
        )
        ocopy[h, "L0"] = send(
            osend.at[h, 0, 0], ofin.at[h, 1, 0], ors.at[h, 3], at_z(3)
        )

    def relay_o(h):
        ocopy[h, "RR"].wait_recv()
        osend[h, 1, 0] = (osend[h, 1, 0].astype(F32) + orel[h, 0].astype(F32)).astype(BF)
        ocopy[h, "R0"] = send(
            osend.at[h, 1, 0], ofin.at[h, 0, 0], ors.at[h, 4], at_z(1)
        )
        ocopy[h, "LL"].wait_recv()
        osend[h, 0, 1] = (osend[h, 0, 1].astype(F32) + orel[h, 1].astype(F32)).astype(BF)
        ocopy[h, "L1"] = send(
            osend.at[h, 0, 1], ofin.at[h, 1, 1], ors.at[h, 5], at_z(3)
        )

    def attend_own(h):
        result = attend(h, (0,))
        num[h] = result[:, :HD]
        tot[h] = result[:, HD:]

    def combine(h):
        for name in ("R0", "R1", "L0", "L1"):
            ocopy[h, name].wait_recv()
        for half in range(2):
            more = ofin[h, 0, half].astype(F32) + ofin[h, 1, half].astype(F32)
            rows = slice(half * BLK, (half + 1) * BLK)
            strip = more[BLK:OROWS]
            total = tot[h, rows, :] + jnp.concatenate([strip] * 16, axis=0).T
            ab[h, 0, rows, :] = ((num[h, rows, :] + more[:BLK]) / total).astype(BF)
        send_ring(ab, acopy, ars, at_x, h)

    def relay_a(h):
        relay_ring(ab, acopy, ars, at_x, h)

    def arrived_a(h):
        arrived_ring(acopy, h)

    def last_rows(pair, side):
        rows = jnp.concatenate([ab[2, pair], ab[2, pair + 1]], axis=1)
        block = jnp.concatenate(
            [wx[pair, side, 2 * HD : COLS, :], wx[pair + 1, side, 2 * HD : COLS, :]], axis=0
        )
        return jnp.dot(rows, block, preferred_element_type=F32)

    def project_first():
        for side in range(2):
            total = None
            for k in range(4):
                rows = jnp.concatenate([ab[0, k], ab[1, k]], axis=1)
                part = jnp.dot(rows, wx[k, side, 0 : 2 * HD, :], preferred_element_type=F32)
                total = part if total is None else total + part
            po[side] = total

    def project_near():
        for side in range(2):
            po[side] = po[side] + last_rows(0, side)

    def finish():
        other = (c + zl + 1) % 2
        given = po[other] + last_rows(2, other)
        zs[...] = given.astype(BF)
        zcopy = send(zs, zr, zrs.at[0], zlo)
        kept = po[1 - other] + last_rows(2, 1 - other)
        sums = given + kept
        turned = (sums[:, :HD] + sums[:, HD : 2 * HD] + sums[:, 2 * HD :]).T
        total = jnp.sum(turned, axis=0, keepdims=True) * D ** (-0.5)
        csb[g] = jnp.broadcast_to(total, (8, SLAB))
        for k in range(1, 8):
            send(csb.at[g], csb.at[g], crs.at[k], (f, (g + k) % 8))
        po[0] = kept
        for k in range(1, 8):
            pltpu.make_async_remote_copy(
                src_ref=csb.at[(g + 8 - k) % 8],
                dst_ref=csb.at[(g + 8 - k) % 8],
                send_sem=pool.at[0],
                recv_sem=crs.at[k],
                device_id=(f, (g + k) % 8),
                device_id_type=MESH,
            ).wait_recv()
        checks = csb[0]
        for k in range(1, 8):
            checks = checks + csb[k]
        cs_ref[...] = checks[0]
        zcopy.wait_recv()
        out_ref[...] = (po[0] + zr[...].astype(F32)).astype(BF)

    def drain(count):
        for i in range(count):
            sent(i)

    make_first()
    pl.semaphore_wait(barrier, len(peers))
    send_t()
    send_kv(0)
    make_q()
    send_q(0)
    make_rest()
    send_q(1)
    make_kv(1)
    send_kv(1)
    for copy in wx_in:
        copy.wait()
    make_kv(2)
    send_w()
    relay_t()
    relay_kv(0)
    send_kv(2)
    relay_q(0)
    send_q(2)
    relay_kv(1)
    last_kv(0)
    relay_q(1)
    limits_table()
    arrived_kv(0)
    attend_sides(0)
    relay_kv(2)
    arrived_q(0)
    attend_opp(0)
    last_kv(1)
    relay_q(2)
    early = len(started)
    arrived_kv(1)
    attend_sides(1)
    last_kv(2)
    arrived_q(1)
    attend_opp(1)
    arrived_kv(2)
    arrived_q(2)
    attend_opp(2)
    attend_sides(2)
    relay_o(0)
    share_w()
    attend_own(0)
    relay_o(1)
    attend_own(1)
    attend_own(2)
    relay_o(2)
    drain(early)
    arrived_w()
    combine(0)
    combine(1)
    relay_a(0)
    combine(2)
    relay_a(1)
    relay_a(2)
    arrived_a(0)
    arrived_a(1)
    project_first()
    project_near()
    arrived_a(2)
    finish()
    drain(len(started))


def place_kernel(rows_ref, sums_ref, rows_hbm, sums_hbm, sem):
    copies = [
        pltpu.make_async_copy(rows_ref, rows_hbm, sem.at[0]),
        pltpu.make_async_copy(sums_ref, sums_hbm, sem.at[1]),
    ]
    for copy in copies:
        copy.start()
    for copy in copies:
        copy.wait()


def per_device(tokens, w_qkv, norm_gains, w_out, near_mask, far_pattern, window):
    any_spec = pl.BlockSpec(memory_space=pl.ANY)
    vmem_spec = pl.BlockSpec(memory_space=pltpu.VMEM)
    dma = pltpu.SemaphoreType.DMA
    held = pl.pallas_call(
        layer_kernel,
        name="layer",
        out_shape=(
            pltpu.VMEM((SLAB, COLS), BF),
            pltpu.VMEM((SLAB,), F32),
        ),
        in_specs=[any_spec] * 7,
        out_specs=(vmem_spec, vmem_spec),
        scratch_shapes=[
            pltpu.VMEM((SLAB, D), BF),
            pltpu.VMEM((HL, D, 2 * HD), BF),
            pltpu.VMEM((D, COLS), BF),
            pltpu.VMEM((4, 2, COLS, COLS), BF),
            pltpu.VMEM((HL, 8, SLAB, 2 * HD), BF),
            pltpu.VMEM((HL, 4, SLAB, HD), BF),
            pltpu.VMEM((2, COLS), F32),
            pltpu.SMEM((2, 4), jnp.int32),
            pltpu.VMEM((2, 64), jnp.int32),
            pltpu.SMEM((32,), jnp.int32),
            pltpu.VMEM((8, 128), jnp.int32),
            pltpu.VMEM((4, 8, 128), F32),
            pltpu.VMEM((8, 32, SLAB), F32),
            pltpu.VMEM((2, BLK, SLAB), F32),
            pltpu.VMEM((2 * SLAB, 8 * SLAB), BF),
            pltpu.VMEM((2 * SLAB, 2 * HD), F32),
            pltpu.VMEM((HL, SLAB, HD), F32),
            pltpu.VMEM((HL, SLAB, HD), F32),
            pltpu.VMEM((HL, 3, 2, OROWS, HD), BF),
            pltpu.VMEM((HL, 2, OROWS, HD), BF),
            pltpu.VMEM((HL, 2, 2, OROWS, HD), BF),
            pltpu.VMEM((HL, 4, SLAB, HD), BF),
            pltpu.VMEM((2, SLAB, COLS), F32),
            pltpu.VMEM((SLAB, COLS), BF),
            pltpu.VMEM((SLAB, COLS), BF),
            pltpu.VMEM((8, 8, SLAB), F32),
            dma((POOL,)),
            dma((HL, 8)),
            dma((HL, 4)),
            dma((3,)),
            dma((7,)),
            dma((HL, 6)),
            dma((HL, 4)),
            dma((1,)),
            dma((8,)),
        ],
        compiler_params=pltpu.CompilerParams(
            collective_id=0, has_side_effects=True, vmem_limit_bytes=56 * 1024 * 1024
        ),
    )(tokens, w_qkv, w_out, norm_gains, near_mask, far_pattern, window)
    return pl.pallas_call(
        place_kernel,
        name="place",
        out_shape=(
            jax.ShapeDtypeStruct((SLAB, COLS), BF),
            jax.ShapeDtypeStruct((SLAB,), F32),
        ),
        in_specs=[vmem_spec, vmem_spec],
        out_specs=(any_spec, any_spec),
        scratch_shapes=[dma((2,))],
    )(*(pltpu.with_memory_space_constraint(part, pltpu.VMEM) for part in held))


def solution(mesh):
    in_specs = (
        P("frame", None),
        P(None, None, "head"),
        P(None, "head"),
        P("head", None),
        P("frame", None),
        P("frame", None),
        P(),
    )
    out_specs = (P("frame", "head"), P("frame"))
    return jax.shard_map(
        per_device, mesh=mesh, in_specs=in_specs, out_specs=out_specs, check_vma=False
    )
```

```python
import jax
import jax.numpy as jnp
from jax import lax
from jax.experimental import pallas as pl
from jax.experimental.pallas import tpu as pltpu
from jax.sharding import PartitionSpec as P

D = 3072
HD = 128
BLK = 128
SLAB = 256
HL = 3
COLS = HL * HD
POOL = 40
PART = 1024
MESH = pl.DeviceIdType.MESH
BF = jnp.bfloat16
F32 = jnp.float32
LOG2E = 1.4426950408889634
OROWS = BLK + 8
NT = (((1,), (1,)), ((), ()))


def layer_kernel(
    tok_hbm,
    w_hbm,
    wo_hbm,
    gains_hbm,
    near_hbm,
    far_hbm,
    window_hbm,
    out_ref,
    cs_ref,
    tok,
    wkv,
    wq,
    wx,
    wo,
    rs,
    csp,
    kv,
    qb,
    gains_ref,
    near_ref,
    far_ref,
    window_ref,
    far,
    tbuf,
    texp,
    dist,
    pbuf,
    acc,
    num,
    tot,
    osend,
    orel,
    ofin,
    ab,
    po,
    zs,
    zr,
    csb,
    pool,
    krs,
    qrs,
    trs,
    wrs,
    ors,
    ars,
    zrs,
    crs,
):
    f = lax.axis_index("frame")
    g = lax.axis_index("head")
    zh, y, c = f // 8, (f // 2) % 4, f % 2
    zl, x = g // 4, g % 4

    def at_y(step):
        return (zh * 8 + ((y + step) % 4) * 2 + c, g)

    def at_z(step):
        return (((zh + step) % 4) * 8 + y * 2 + c, g)

    def at_x(step):
        return (f, zl * 4 + (x + step) % 4)

    core = (zh * 8 + y * 2 + (1 - c), g)
    zlo = (f, (1 - zl) * 4 + x)

    started = []
    waited = set()

    def sent(i):
        if i not in waited:
            waited.add(i)
            started[i].wait_send()

    def send(src, dst, rsem, dev):
        n = len(started)
        if n >= POOL:
            sent(n - POOL)
        copy = pltpu.make_async_remote_copy(
            src_ref=src,
            dst_ref=dst,
            send_sem=pool.at[n % POOL],
            recv_sem=rsem,
            device_id=dev,
            device_id_type=MESH,
        )
        copy.start()
        started.append(copy)
        return copy

    def fetch(src, dst, i):
        copy = pltpu.make_async_copy(src, dst, pool.at[POOL - 22 + i])
        copy.start()
        return copy

    def columns(side, step):
        at = (side * 4 + (x + step) % 4) * COLS
        return pl.ds(pl.multiple_of(at, HD), COLS)

    barrier = pltpu.get_barrier_semaphore()
    peers = [at_y(1), at_y(3), core, at_z(1), at_z(3)]
    peers += [(f, (g + k) % 8) for k in range(1, 8)]
    for peer in peers:
        pl.semaphore_signal(barrier, inc=1, device_id=peer, device_id_type=MESH)

    small_in = [
        fetch(near_hbm, near_ref, 10),
        fetch(window_hbm, window_ref, 11),
        fetch(far_hbm, far_ref, 12),
        fetch(gains_hbm, gains_ref, 13),
    ]
    kv_in = []
    for k in range(3):
        span = pl.ds(k * PART, PART)
        kv_in.append(
            (
                fetch(tok_hbm.at[:, span], tok.at[:, span], 3 * k),
                fetch(w_hbm.at[1, span, pl.ds(0, HD)], wkv.at[0, span, pl.ds(0, HD)], 3 * k + 1),
                fetch(w_hbm.at[2, span, pl.ds(0, HD)], wkv.at[0, span, pl.ds(HD, HD)], 3 * k + 2),
            )
        )
    first, rest = pl.ds(0, HD), pl.ds(HD, 2 * HD)
    q_first = fetch(w_hbm.at[0, :, first], wq.at[:, first], 14)
    q_rest = fetch(w_hbm.at[0, :, rest], wq.at[:, rest], 15)
    later_in = {}
    for h in (1, 2):
        hs = pl.ds(h * HD, HD)
        later_in[h] = (
            fetch(w_hbm.at[1, :, hs], wkv.at[h, :, pl.ds(0, HD)], 14 + 2 * h),
            fetch(w_hbm.at[2, :, hs], wkv.at[h, :, pl.ds(HD, HD)], 15 + 2 * h),
        )
    wx_in = (
        fetch(wo_hbm.at[:, columns(c, 0)], wx.at[0, 0], 9),
        fetch(wo_hbm.at[:, columns(1 - c, 0)], wx.at[0, 1], 20),
        fetch(wo_hbm, wo, 21),
    )

    for copy in small_in:
        copy.wait()
    lane = lax.broadcasted_iota(jnp.int32, (8, 128), 1)
    line = lax.broadcasted_iota(jnp.int32, (8, 128), 0)
    slabs = lax.shift_right_logical(lane, 1)
    odd = lane - 2 * slabs
    apart = jnp.abs(slabs - f)
    limits = jnp.zeros((8, 128), jnp.int32)
    for d in range(32):
        limits = jnp.where(apart == d, window_ref[d], limits)
    near = []
    for a in range(2):
        before = jnp.where(odd == 1, near_ref[a, 1], near_ref[a, 0])
        after = jnp.where(odd == 1, near_ref[a, 3], near_ref[a, 2])
        near.append(jnp.where(slabs < f, before, after))
    far[...] = jnp.zeros((8, 128), jnp.int32)
    far[0:2, 0:64] = far_ref[...]
    chosen = jnp.where(apart == 1, jnp.where(line == 0, near[0], near[1]), far[...])
    chosen = jnp.where(apart == 0, 1, chosen)
    tbuf[0] = jnp.where(chosen > 0, limits, 0).astype(F32)

    def keep_kv(h, both):
        key = both[:, :HD]
        factor = lax.rsqrt(jnp.mean(key * key, axis=1, keepdims=True) + 1e-06)
        gain = gains_ref[1:2, h * HD : (h + 1) * HD]
        kv[h, 0, :, 0:HD] = (key * factor * gain).astype(BF)
        kv[h, 0, :, HD : 2 * HD] = both[:, HD:].astype(BF)

    def make_first():
        both = None
        for k in range(3):
            for copy in kv_in[k]:
                copy.wait()
            span = slice(k * PART, (k + 1) * PART)
            part = jnp.dot(tok[:, span], wkv[0, span, :], preferred_element_type=F32)
            both = part if both is None else both + part
        keep_kv(0, both)

    def make_kv(h):
        for copy in later_in[h]:
            copy.wait()
        keep_kv(h, jnp.dot(tok[...], wkv[h], preferred_element_type=F32))

    def keep_q(h, query):
        factor = lax.rsqrt(jnp.mean(query * query, axis=1, keepdims=True) + 1e-06)
        gain = gains_ref[0:1, h * HD : (h + 1) * HD] * (HD**-0.5 * LOG2E)
        qb[h, 0] = (query * factor * gain).astype(BF)

    def make_q():
        q_first.wait()
        keep_q(0, jnp.dot(tok[...], wq[:, 0:HD], preferred_element_type=F32))

    def make_rest():
        q_rest.wait()
        both = jnp.dot(tok[...], wq[:, HD:], preferred_element_type=F32)
        keep_q(1, both[:, :HD])
        keep_q(2, both[:, HD:])

    top, low = pl.ds(0, BLK), pl.ds(BLK, BLK)
    kcopy, qcopy, tcopy, wcopy, ocopy, acopy = {}, {}, {}, {}, {}, {}

    def send_kv(h):
        own = kv.at[h, 0]
        kcopy[h, "R"] = send(own, kv.at[h, 1], krs.at[h, 0], at_y(1))
        kcopy[h, "L"] = send(own, kv.at[h, 2], krs.at[h, 1], at_y(3))
        kcopy[h, "c0"] = send(own, kv.at[h, 4], krs.at[h, 2], core)

    def relay_kv(h):
        kcopy[h, "R"].wait_recv()
        kcopy[h, "RR"] = send(
            kv.at[h, 1, top], kv.at[h, 3, top], krs.at[h, 3], at_y(1)
        )
        kcopy[h, "c1"] = send(kv.at[h, 1], kv.at[h, 5], krs.at[h, 4], core)
        kcopy[h, "L"].wait_recv()
        kcopy[h, "LL"] = send(
            kv.at[h, 2, low], kv.at[h, 3, low], krs.at[h, 5], at_y(3)
        )
        kcopy[h, "c2"] = send(kv.at[h, 2], kv.at[h, 6], krs.at[h, 6], core)

    def last_kv(h):
        kcopy[h, "RR"].wait_recv()
        kcopy[h, "LL"].wait_recv()
        kcopy[h, "c3"] = send(kv.at[h, 3], kv.at[h, 7], krs.at[h, 7], core)

    def arrived_kv(h):
        for name in ("c0", "c1", "c2", "c3"):
            kcopy[h, name].wait_recv()

    def send_ring(buf, copies, rsem, to, h):
        own = buf.at[h, 0]
        copies[h, "R"] = send(own, buf.at[h, 1], rsem.at[h, 0], to(1))
        copies[h, "L"] = send(own, buf.at[h, 2], rsem.at[h, 1], to(3))

    def relay_ring(buf, copies, rsem, to, h):
        copies[h, "R"].wait_recv()
        copies[h, "RR"] = send(
            buf.at[h, 1, top], buf.at[h, 3, top], rsem.at[h, 2], to(1)
        )
        copies[h, "L"].wait_recv()
        copies[h, "LL"] = send(
            buf.at[h, 2, low], buf.at[h, 3, low], rsem.at[h, 3], to(3)
        )

    def arrived_ring(copies, h):
        copies[h, "RR"].wait_recv()
        copies[h, "LL"].wait_recv()

    def send_q(h):
        send_ring(qb, qcopy, qrs, at_z, h)

    def relay_q(h):
        relay_ring(qb, qcopy, qrs, at_z, h)

    def arrived_q(h):
        arrived_ring(qcopy, h)

    def send_t():
        tcopy["R"] = send(tbuf.at[0], tbuf.at[1], trs.at[0], at_z(1))
        tcopy["L"] = send(tbuf.at[0], tbuf.at[2], trs.at[1], at_z(3))

    def relay_t():
        tcopy["R"].wait_recv()
        tcopy["RR"] = send(tbuf.at[1], tbuf.at[3], trs.at[2], at_z(1))
        tcopy["L"].wait_recv()

    def send_w():
        for k, step in ((1, 1), (2, 3), (3, 2)):
            wcopy[k] = send(
                wo_hbm.at[:, columns(c, step)], wx.at[k, 0], wrs.at[k], at_x(step)
            )

    def share_w():
        for k in (1, 2, 3):
            wcopy[k].wait_recv()
            wcopy[k + 3] = send(wx.at[k, 0], wx.at[k, 1], wrs.at[k + 3], core)

    def arrived_w():
        for k in (4, 5, 6):
            wcopy[k].wait_recv()

    def limits_table():
        row = lax.broadcasted_iota(jnp.int32, (BLK, SLAB), 0)
        col = lax.broadcasted_iota(jnp.int32, (BLK, SLAB), 1)
        for rh in range(2):
            dist[rh] = jnp.abs(row + rh * BLK - col).astype(F32)
        tcopy["RR"].wait_recv()
        table = tbuf[...].reshape(4 * 8, 128).astype(BF)
        half = (col >= BLK).astype(jnp.int32)
        for j in range(8):
            slab = zh * 8 + ((y + (0, 3, 1, 2)[j % 4]) % 4) * 2 + (c if j < 4 else 1 - c)
            pick = (row == half + slab * 2).astype(F32).astype(BF)
            texp[j] = jnp.dot(table, pick, preferred_element_type=F32)

    def row_sums():
        whole = jnp.dot(wo[...], jnp.ones((D, HD), BF), preferred_element_type=F32)
        high = whole.astype(BF)
        rs[:, 0:HD] = high
        rs[:, HD:] = (whole - high.astype(F32)).astype(BF)

    def attend(h, slots):
        size = SLAB * len(slots)
        queries = jnp.concatenate([qb[h, q] for q in slots], axis=0)

        for k in range(4):
            pair = slice(2 * k, 2 * k + 2)
            cols = slice(2 * k * SLAB, (2 * k + 2) * SLAB)
            for j in range(2 * k, 2 * k + 2):
                raw = lax.dot_general(queries, kv[h, j, :, 0:HD], NT, preferred_element_type=F32)
                for i, q in enumerate(slots):
                    for rh in range(2):
                        rows = slice(i * SLAB + rh * BLK, i * SLAB + (rh + 1) * BLK)
                        limit = texp[j, q * 8 + rh : q * 8 + rh + 1, :]
                        weight = jnp.where(dist[rh] < limit, jnp.exp2(raw[rows]), 0.0)
                        pbuf[rows, j * SLAB : (j + 1) * SLAB] = weight.astype(BF)
            values = kv[h, pair, :, HD : 2 * HD].reshape(2 * SLAB, HD)
            values = jnp.concatenate([values, jnp.ones((2 * SLAB, HD), BF)], axis=1)
            part = jnp.dot(pbuf[0:size, cols], values, preferred_element_type=F32)
            if k == 0:
                acc[0:size, :] = part
            else:
                acc[0:size, :] += part
        return acc[0:size, :]

    def pack(h, dest, part):
        for half in range(2):
            rows = part[half * BLK : (half + 1) * BLK]
            osend[h, dest, half, 0:BLK, :] = rows[:, :HD].astype(BF)
            osend[h, dest, half, BLK:OROWS, :] = rows[:, HD:].T[0:8].astype(BF)

    def attend_opp(h):
        pack(h, 2, attend(h, (3,)))
        ocopy[h, "RR"] = send(
            osend.at[h, 2, 0], orel.at[h, 0], ors.at[h, 0], at_z(1)
        )
        ocopy[h, "LL"] = send(
            osend.at[h, 2, 1], orel.at[h, 1], ors.at[h, 1], at_z(3)
        )

    def attend_sides(h):
        result = attend(h, (1, 2))
        pack(h, 0, result[:SLAB])
        pack(h, 1, result[SLAB:])
        ocopy[h, "R1"] = send(
            osend.at[h, 1, 1], ofin.at[h, 0, 1], ors.at[h, 2], at_z(1)
        )
        ocopy[h, "L0"] = send(
            osend.at[h, 0, 0], ofin.at[h, 1, 0], ors.at[h, 3], at_z(3)
        )

    def relay_o(h):
        ocopy[h, "RR"].wait_recv()
        osend[h, 1, 0] = (osend[h, 1, 0].astype(F32) + orel[h, 0].astype(F32)).astype(BF)
        ocopy[h, "R0"] = send(
            osend.at[h, 1, 0], ofin.at[h, 0, 0], ors.at[h, 4], at_z(1)
        )
        ocopy[h, "LL"].wait_recv()
        osend[h, 0, 1] = (osend[h, 0, 1].astype(F32) + orel[h, 1].astype(F32)).astype(BF)
        ocopy[h, "L1"] = send(
            osend.at[h, 0, 1], ofin.at[h, 1, 1], ors.at[h, 5], at_z(3)
        )

    def attend_own(h):
        result = attend(h, (0,))
        num[h] = result[:, :HD]
        tot[h] = result[:, HD:]

    def combine(h):
        for name in ("R0", "R1", "L0", "L1"):
            ocopy[h, name].wait_recv()
        for half in range(2):
            more = ofin[h, 0, half].astype(F32) + ofin[h, 1, half].astype(F32)
            rows = slice(half * BLK, (half + 1) * BLK)
            strip = more[BLK:OROWS]
            total = tot[h, rows, :] + jnp.concatenate([strip] * 16, axis=0).T
            ab[h, 0, rows, :] = ((num[h, rows, :] + more[:BLK]) / total).astype(BF)
            if h == 2:
                part = (top, low)[half]
                own = ab.at[h, 0, part]
                acopy[h, "R", half] = send(own, ab.at[h, 1, part], ars.at[h, half], at_x(1))
                acopy[h, "L", half] = send(own, ab.at[h, 2, part], ars.at[h, 2 + half], at_x(3))
        if h < 2:
            send_ring(ab, acopy, ars, at_x, h)
        both = jnp.dot(ab[h, 0], rs[h * HD : (h + 1) * HD, :], preferred_element_type=F32)
        if h == 0:
            csp[...] = both[:, :HD] + both[:, HD:]
        else:
            csp[...] += both[:, :HD] + both[:, HD:]

    def relay_last():
        acopy[2, "R", 0].wait_recv()
        acopy[2, "RR"] = send(ab.at[2, 1, top], ab.at[2, 3, top], ars.at[2, 4], at_x(1))
        acopy[2, "L", 1].wait_recv()
        acopy[2, "LL"] = send(ab.at[2, 2, low], ab.at[2, 3, low], ars.at[2, 5], at_x(3))

    def send_checks():
        csb[g] = (csp[...] * D ** (-0.5)).T[0:8]
        for k in range(1, 8):
            send(csb.at[g], csb.at[g], crs.at[k], (f, (g + k) % 8))

    def relay_a(h):
        relay_ring(ab, acopy, ars, at_x, h)

    def arrived_a(h):
        arrived_ring(acopy, h)

    def last_rows(half, side):
        part = slice(half * BLK, (half + 1) * BLK)
        rows = jnp.concatenate([ab[2, k, part, :] for k in range(4)], axis=1)
        block = jnp.concatenate([wx[k, side, 2 * HD : COLS, :] for k in range(4)], axis=0)
        return po[side, part, :] + jnp.dot(rows, block, preferred_element_type=F32)

    def project_first():
        for side in range(2):
            total = None
            for k in range(4):
                rows = jnp.concatenate([ab[0, k], ab[1, k]], axis=1)
                part = jnp.dot(rows, wx[k, side, 0 : 2 * HD, :], preferred_element_type=F32)
                total = part if total is None else total + part
            po[side] = total

    def close_checks():
        for k in range(1, 8):
            pltpu.make_async_remote_copy(
                src_ref=csb.at[(g + 8 - k) % 8],
                dst_ref=csb.at[(g + 8 - k) % 8],
                send_sem=pool.at[0],
                recv_sem=crs.at[k],
                device_id=(f, (g + k) % 8),
                device_id_type=MESH,
            ).wait_recv()
        checks = csb[0]
        for k in range(1, 8):
            checks = checks + csb[k]
        cs_ref[...] = checks[0]

    def drain(count):
        for i in range(count):
            sent(i)

    def finish():
        other = (c + zl + 1) % 2
        zcopy = []
        for half in range(2):
            if half == 0:
                acopy[2, "L", 0].wait_recv()
                acopy[2, "RR"].wait_recv()
            else:
                acopy[2, "R", 1].wait_recv()
                acopy[2, "LL"].wait_recv()
            part = (top, low)[half]
            zs[part, :] = last_rows(half, other).astype(BF)
            zcopy.append(send(zs.at[part], zr.at[part], zrs.at[half], zlo))
        kept = [last_rows(half, 1 - other) for half in range(2)]
        drain(len(started) - 2)
        for half in range(2):
            rows = slice(half * BLK, (half + 1) * BLK)
            zcopy[half].wait_recv()
            out_ref[rows, :] = (kept[half] + zr[rows, :].astype(F32)).astype(BF)

    make_first()
    pl.semaphore_wait(barrier, len(peers))
    send_t()
    send_kv(0)
    make_q()
    send_q(0)
    make_rest()
    send_q(1)
    send_q(2)
    make_kv(1)
    send_kv(1)
    make_kv(2)
    for copy in wx_in:
        copy.wait()
    send_w()
    relay_t()
    relay_kv(0)
    send_kv(2)
    row_sums()
    last_kv(0)
    relay_kv(1)
    relay_q(0)
    relay_q(1)
    limits_table()
    arrived_kv(0)
    attend_sides(0)
    relay_kv(2)
    relay_q(2)
    last_kv(1)
    arrived_q(0)
    attend_opp(0)
    early = len(started)
    arrived_kv(1)
    attend_sides(1)
    last_kv(2)
    arrived_q(1)
    attend_opp(1)
    relay_o(0)
    arrived_kv(2)
    arrived_q(2)
    attend_opp(2)
    attend_own(0)
    attend_sides(2)
    relay_o(1)
    share_w()
    attend_own(1)
    attend_own(2)
    combine(0)
    relay_o(2)
    drain(early)
    arrived_w()
    combine(1)
    relay_a(0)
    combine(2)
    send_checks()
    relay_a(1)
    relay_last()
    arrived_a(0)
    arrived_a(1)
    project_first()
    close_checks()
    finish()
    drain(len(started))


def place_kernel(rows_ref, sums_ref, rows_hbm, sums_hbm, sem):
    copies = [
        pltpu.make_async_copy(rows_ref, rows_hbm, sem.at[0]),
        pltpu.make_async_copy(sums_ref, sums_hbm, sem.at[1]),
    ]
    for copy in copies:
        copy.start()
    for copy in copies:
        copy.wait()


def per_device(tokens, w_qkv, norm_gains, w_out, near_mask, far_pattern, window):
    any_spec = pl.BlockSpec(memory_space=pl.ANY)
    vmem_spec = pl.BlockSpec(memory_space=pltpu.VMEM)
    dma = pltpu.SemaphoreType.DMA
    held = pl.pallas_call(
        layer_kernel,
        name="layer",
        out_shape=(
            pltpu.VMEM((SLAB, COLS), BF),
            pltpu.VMEM((SLAB,), F32),
        ),
        in_specs=[any_spec] * 7,
        out_specs=(vmem_spec, vmem_spec),
        scratch_shapes=[
            pltpu.VMEM((SLAB, D), BF),
            pltpu.VMEM((HL, D, 2 * HD), BF),
            pltpu.VMEM((D, COLS), BF),
            pltpu.VMEM((4, 2, COLS, COLS), BF),
            pltpu.VMEM((COLS, D), BF),
            pltpu.VMEM((COLS, 2 * HD), BF),
            pltpu.VMEM((SLAB, HD), F32),
            pltpu.VMEM((HL, 8, SLAB, 2 * HD), BF),
            pltpu.VMEM((HL, 4, SLAB, HD), BF),
            pltpu.VMEM((2, COLS), F32),
            pltpu.SMEM((2, 4), jnp.int32),
            pltpu.VMEM((2, 64), jnp.int32),
            pltpu.SMEM((32,), jnp.int32),
            pltpu.VMEM((8, 128), jnp.int32),
            pltpu.VMEM((4, 8, 128), F32),
            pltpu.VMEM((8, 32, SLAB), F32),
            pltpu.VMEM((2, BLK, SLAB), F32),
            pltpu.VMEM((2 * SLAB, 8 * SLAB), BF),
            pltpu.VMEM((2 * SLAB, 2 * HD), F32),
            pltpu.VMEM((HL, SLAB, HD), F32),
            pltpu.VMEM((HL, SLAB, HD), F32),
            pltpu.VMEM((HL, 3, 2, OROWS, HD), BF),
            pltpu.VMEM((HL, 2, OROWS, HD), BF),
            pltpu.VMEM((HL, 2, 2, OROWS, HD), BF),
            pltpu.VMEM((HL, 4, SLAB, HD), BF),
            pltpu.VMEM((2, SLAB, COLS), F32),
            pltpu.VMEM((SLAB, COLS), BF),
            pltpu.VMEM((SLAB, COLS), BF),
            pltpu.VMEM((8, 8, SLAB), F32),
            dma((POOL,)),
            dma((HL, 8)),
            dma((HL, 4)),
            dma((3,)),
            dma((7,)),
            dma((HL, 6)),
            dma((HL, 6)),
            dma((2,)),
            dma((8,)),
        ],
        compiler_params=pltpu.CompilerParams(
            collective_id=0, has_side_effects=True, vmem_limit_bytes=56 * 1024 * 1024
        ),
    )(tokens, w_qkv, w_out, norm_gains, near_mask, far_pattern, window)
    return pl.pallas_call(
        place_kernel,
        name="place",
        out_shape=(
            jax.ShapeDtypeStruct((SLAB, COLS), BF),
            jax.ShapeDtypeStruct((SLAB,), F32),
        ),
        in_specs=[vmem_spec, vmem_spec],
        out_specs=(any_spec, any_spec),
        scratch_shapes=[dma((2,))],
    )(*(pltpu.with_memory_space_constraint(part, pltpu.VMEM) for part in held))


def solution(mesh):
    in_specs = (
        P("frame", None),
        P(None, None, "head"),
        P(None, "head"),
        P("head", None),
        P("frame", None),
        P("frame", None),
        P(),
    )
    out_specs = (P("frame", "head"), P("frame"))
    return jax.shard_map(
        per_device, mesh=mesh, in_specs=in_specs, out_specs=out_specs, check_vma=False
    )
```

```python
import jax
import jax.numpy as jnp
from jax import lax
from jax.experimental import pallas as pl
from jax.experimental.pallas import tpu as pltpu
from jax.sharding import PartitionSpec as P

D = 3072
HD = 128
BLK = 128
SLAB = 256
HL = 3
COLS = HL * HD
POOL = 40
PART = 1024
MESH = pl.DeviceIdType.MESH
BF = jnp.bfloat16
F32 = jnp.float32
LOG2E = 1.4426950408889634
OROWS = BLK + 8
NT = (((1,), (1,)), ((), ()))


def layer_body(
    pool,
    krs,
    qrs,
    trs,
    wrs,
    ors,
    ars,
    zrs,
    crs,
    tok_hbm,
    w_hbm,
    wo_hbm,
    gains_hbm,
    near_hbm,
    far_hbm,
    window_hbm,
    out_ref,
    cs_ref,
    tok,
    wkv,
    wq,
    wx,
    wo,
    rs,
    csp,
    kv,
    qb,
    gains_ref,
    near_ref,
    far_ref,
    window_ref,
    far,
    tbuf,
    texp,
    dist,
    pbuf,
    acc,
    num,
    tot,
    osend,
    orel,
    ofin,
    ab,
    po,
    zs,
    zr,
    csb,
):
    f = lax.axis_index("frame")
    g = lax.axis_index("head")
    zh, y, c = f // 8, (f // 2) % 4, f % 2
    zl, x = g // 4, g % 4

    def at_y(step):
        return (zh * 8 + ((y + step) % 4) * 2 + c, g)

    def at_z(step):
        return (((zh + step) % 4) * 8 + y * 2 + c, g)

    def at_x(step):
        return (f, zl * 4 + (x + step) % 4)

    core = (zh * 8 + y * 2 + (1 - c), g)
    zlo = (f, (1 - zl) * 4 + x)

    started = []
    waited = set()

    def sent(i):
        if i not in waited:
            waited.add(i)
            started[i].wait_send()

    def send(src, dst, rsem, dev):
        n = len(started)
        if n >= POOL:
            sent(n - POOL)
        copy = pltpu.make_async_remote_copy(
            src_ref=src,
            dst_ref=dst,
            send_sem=pool.at[n % POOL],
            recv_sem=rsem,
            device_id=dev,
            device_id_type=MESH,
        )
        copy.start()
        started.append(copy)
        return copy

    def fetch(src, dst, i):
        copy = pltpu.make_async_copy(src, dst, pool.at[POOL - 22 + i])
        copy.start()
        return copy

    def columns(side, step):
        at = (side * 4 + (x + step) % 4) * COLS
        return pl.ds(pl.multiple_of(at, HD), COLS)

    small_in = [
        fetch(near_hbm, near_ref, 10),
        fetch(window_hbm, window_ref, 11),
        fetch(far_hbm, far_ref, 12),
        fetch(gains_hbm, gains_ref, 13),
    ]
    kv_in = []
    for k in range(3):
        span = pl.ds(k * PART, PART)
        kv_in.append(
            (
                fetch(tok_hbm.at[:, span], tok.at[:, span], 3 * k),
                fetch(w_hbm.at[1, span, pl.ds(0, HD)], wkv.at[0, span, pl.ds(0, HD)], 3 * k + 1),
                fetch(w_hbm.at[2, span, pl.ds(0, HD)], wkv.at[0, span, pl.ds(HD, HD)], 3 * k + 2),
            )
        )
    barrier = pltpu.get_barrier_semaphore()
    peers = [at_y(1), at_y(3), core, at_z(1), at_z(3)]
    peers += [(f, (g + k) % 8) for k in range(1, 8)]
    for peer in peers:
        pl.semaphore_signal(barrier, inc=1, device_id=peer, device_id_type=MESH)

    first, rest = pl.ds(0, HD), pl.ds(HD, 2 * HD)
    q_first = fetch(w_hbm.at[0, :, first], wq.at[:, first], 14)
    q_rest = fetch(w_hbm.at[0, :, rest], wq.at[:, rest], 15)
    later_in = {}
    for h in (1, 2):
        hs = pl.ds(h * HD, HD)
        later_in[h] = (
            fetch(w_hbm.at[1, :, hs], wkv.at[h, :, pl.ds(0, HD)], 14 + 2 * h),
            fetch(w_hbm.at[2, :, hs], wkv.at[h, :, pl.ds(HD, HD)], 15 + 2 * h),
        )
    wx_in = (
        fetch(wo_hbm.at[:, columns(c, 0)], wx.at[0, 0], 9),
        fetch(wo_hbm.at[:, columns(1 - c, 0)], wx.at[0, 1], 20),
        fetch(wo_hbm, wo, 21),
    )

    for copy in small_in:
        copy.wait()
    lane = lax.broadcasted_iota(jnp.int32, (8, 128), 1)
    line = lax.broadcasted_iota(jnp.int32, (8, 128), 0)
    slabs = lax.shift_right_logical(lane, 1)
    odd = lane - 2 * slabs
    apart = jnp.abs(slabs - f)
    limits = jnp.zeros((8, 128), jnp.int32)
    for d in range(32):
        limits = jnp.where(apart == d, window_ref[d], limits)
    near = []
    for a in range(2):
        before = jnp.where(odd == 1, near_ref[a, 1], near_ref[a, 0])
        after = jnp.where(odd == 1, near_ref[a, 3], near_ref[a, 2])
        near.append(jnp.where(slabs < f, before, after))
    far[...] = jnp.zeros((8, 128), jnp.int32)
    far[0:2, 0:64] = far_ref[...]
    chosen = jnp.where(apart == 1, jnp.where(line == 0, near[0], near[1]), far[...])
    chosen = jnp.where(apart == 0, 1, chosen)
    tbuf[0] = jnp.where(chosen > 0, limits, 0).astype(F32)

    def keep_kv(h, both):
        key = both[:, :HD]
        factor = lax.rsqrt(jnp.mean(key * key, axis=1, keepdims=True) + 1e-06)
        gain = gains_ref[1:2, h * HD : (h + 1) * HD]
        kv[h, 0, :, 0:HD] = (key * factor * gain).astype(BF)
        kv[h, 0, :, HD : 2 * HD] = both[:, HD:].astype(BF)

    def make_first():
        both = None
        for k in range(3):
            for copy in kv_in[k]:
                copy.wait()
            span = slice(k * PART, (k + 1) * PART)
            part = jnp.dot(tok[:, span], wkv[0, span, :], preferred_element_type=F32)
            both = part if both is None else both + part
        keep_kv(0, both)

    def make_kv(h):
        for copy in later_in[h]:
            copy.wait()
        keep_kv(h, jnp.dot(tok[...], wkv[h], preferred_element_type=F32))

    def keep_q(h, query):
        factor = lax.rsqrt(jnp.mean(query * query, axis=1, keepdims=True) + 1e-06)
        gain = gains_ref[0:1, h * HD : (h + 1) * HD] * (HD**-0.5 * LOG2E)
        qb[h, 0] = (query * factor * gain).astype(BF)

    def make_q():
        q_first.wait()
        keep_q(0, jnp.dot(tok[...], wq[:, 0:HD], preferred_element_type=F32))

    def make_rest():
        q_rest.wait()
        both = jnp.dot(tok[...], wq[:, HD:], preferred_element_type=F32)
        keep_q(1, both[:, :HD])
        keep_q(2, both[:, HD:])

    top, low = pl.ds(0, BLK), pl.ds(BLK, BLK)
    kcopy, qcopy, tcopy, wcopy, ocopy, acopy = {}, {}, {}, {}, {}, {}

    def send_kv(h):
        own = kv.at[h, 0]
        kcopy[h, "R"] = send(own, kv.at[h, 1], krs.at[h, 0], at_y(1))
        kcopy[h, "L"] = send(own, kv.at[h, 2], krs.at[h, 1], at_y(3))
        kcopy[h, "c0"] = send(own, kv.at[h, 4], krs.at[h, 2], core)

    def relay_kv(h):
        kcopy[h, "R"].wait_recv()
        kcopy[h, "RR"] = send(
            kv.at[h, 1, top], kv.at[h, 3, top], krs.at[h, 3], at_y(1)
        )
        kcopy[h, "c1"] = send(kv.at[h, 1], kv.at[h, 5], krs.at[h, 4], core)
        kcopy[h, "L"].wait_recv()
        kcopy[h, "LL"] = send(
            kv.at[h, 2, low], kv.at[h, 3, low], krs.at[h, 5], at_y(3)
        )
        kcopy[h, "c2"] = send(kv.at[h, 2], kv.at[h, 6], krs.at[h, 6], core)

    def last_kv(h):
        kcopy[h, "RR"].wait_recv()
        kcopy[h, "LL"].wait_recv()
        kcopy[h, "c3"] = send(kv.at[h, 3], kv.at[h, 7], krs.at[h, 7], core)

    def arrived_kv(h):
        for name in ("c0", "c1", "c2", "c3"):
            kcopy[h, name].wait_recv()

    def send_ring(buf, copies, rsem, to, h):
        own = buf.at[h, 0]
        copies[h, "R"] = send(own, buf.at[h, 1], rsem.at[h, 0], to(1))
        copies[h, "L"] = send(own, buf.at[h, 2], rsem.at[h, 1], to(3))

    def relay_ring(buf, copies, rsem, to, h):
        copies[h, "R"].wait_recv()
        copies[h, "RR"] = send(
            buf.at[h, 1, top], buf.at[h, 3, top], rsem.at[h, 2], to(1)
        )
        copies[h, "L"].wait_recv()
        copies[h, "LL"] = send(
            buf.at[h, 2, low], buf.at[h, 3, low], rsem.at[h, 3], to(3)
        )

    def arrived_ring(copies, h):
        copies[h, "RR"].wait_recv()
        copies[h, "LL"].wait_recv()

    def send_q(h):
        send_ring(qb, qcopy, qrs, at_z, h)

    def relay_q(h):
        relay_ring(qb, qcopy, qrs, at_z, h)

    def arrived_q(h):
        arrived_ring(qcopy, h)

    def send_t():
        tcopy["R"] = send(tbuf.at[0], tbuf.at[1], trs.at[0], at_z(1))
        tcopy["L"] = send(tbuf.at[0], tbuf.at[2], trs.at[1], at_z(3))

    def relay_t():
        tcopy["R"].wait_recv()
        tcopy["RR"] = send(tbuf.at[1], tbuf.at[3], trs.at[2], at_z(1))
        tcopy["L"].wait_recv()

    def send_w():
        for k, step in ((1, 1), (2, 3), (3, 2)):
            wcopy[k] = send(
                wo_hbm.at[:, columns(c, step)], wx.at[k, 0], wrs.at[k], at_x(step)
            )

    def share_w():
        for k in (1, 2, 3):
            wcopy[k].wait_recv()
            wcopy[k + 3] = send(wx.at[k, 0], wx.at[k, 1], wrs.at[k + 3], core)

    def arrived_w():
        for k in (4, 5, 6):
            wcopy[k].wait_recv()

    def limits_table():
        row = lax.broadcasted_iota(jnp.int32, (BLK, SLAB), 0)
        col = lax.broadcasted_iota(jnp.int32, (BLK, SLAB), 1)
        for rh in range(2):
            dist[rh] = jnp.abs(row + rh * BLK - col).astype(F32)
        tcopy["RR"].wait_recv()
        table = tbuf[...].reshape(4 * 8, 128).astype(BF)
        half = (col >= BLK).astype(jnp.int32)
        for j in range(8):
            slab = zh * 8 + ((y + (0, 3, 1, 2)[j % 4]) % 4) * 2 + (c if j < 4 else 1 - c)
            pick = (row == half + slab * 2).astype(F32).astype(BF)
            texp[j] = jnp.dot(table, pick, preferred_element_type=F32)

    def row_sums():
        whole = jnp.dot(wo[...], jnp.ones((D, HD), BF), preferred_element_type=F32)
        high = whole.astype(BF)
        rs[:, 0:HD] = high
        rs[:, HD:] = (whole - high.astype(F32)).astype(BF)

    def attend(h, slots):
        size = SLAB * len(slots)
        queries = jnp.concatenate([qb[h, q] for q in slots], axis=0)

        for k in range(4):
            pair = slice(2 * k, 2 * k + 2)
            cols = slice(2 * k * SLAB, (2 * k + 2) * SLAB)
            for j in range(2 * k, 2 * k + 2):
                raw = lax.dot_general(queries, kv[h, j, :, 0:HD], NT, preferred_element_type=F32)
                for i, q in enumerate(slots):
                    for rh in range(2):
                        rows = slice(i * SLAB + rh * BLK, i * SLAB + (rh + 1) * BLK)
                        limit = texp[j, q * 8 + rh : q * 8 + rh + 1, :]
                        weight = jnp.where(dist[rh] < limit, jnp.exp2(raw[rows]), 0.0)
                        pbuf[rows, j * SLAB : (j + 1) * SLAB] = weight.astype(BF)
            values = kv[h, pair, :, HD : 2 * HD].reshape(2 * SLAB, HD)
            values = jnp.concatenate([values, jnp.ones((2 * SLAB, HD), BF)], axis=1)
            part = jnp.dot(pbuf[0:size, cols], values, preferred_element_type=F32)
            if k == 0:
                acc[0:size, :] = part
            else:
                acc[0:size, :] += part
        return acc[0:size, :]

    def pack(h, dest, part):
        for half in range(2):
            rows = part[half * BLK : (half + 1) * BLK]
            osend[h, dest, half, 0:BLK, :] = rows[:, :HD].astype(BF)
            osend[h, dest, half, BLK:OROWS, :] = rows[:, HD:].T[0:8].astype(BF)

    def attend_opp(h):
        pack(h, 2, attend(h, (3,)))
        ocopy[h, "RR"] = send(
            osend.at[h, 2, 0], orel.at[h, 0], ors.at[h, 0], at_z(1)
        )
        ocopy[h, "LL"] = send(
            osend.at[h, 2, 1], orel.at[h, 1], ors.at[h, 1], at_z(3)
        )

    def attend_sides(h):
        result = attend(h, (1, 2))
        pack(h, 0, result[:SLAB])
        pack(h, 1, result[SLAB:])
        ocopy[h, "R1"] = send(
            osend.at[h, 1, 1], ofin.at[h, 0, 1], ors.at[h, 2], at_z(1)
        )
        ocopy[h, "L0"] = send(
            osend.at[h, 0, 0], ofin.at[h, 1, 0], ors.at[h, 3], at_z(3)
        )

    def relay_o(h):
        ocopy[h, "RR"].wait_recv()
        osend[h, 1, 0] = (osend[h, 1, 0].astype(F32) + orel[h, 0].astype(F32)).astype(BF)
        ocopy[h, "R0"] = send(
            osend.at[h, 1, 0], ofin.at[h, 0, 0], ors.at[h, 4], at_z(1)
        )
        ocopy[h, "LL"].wait_recv()
        osend[h, 0, 1] = (osend[h, 0, 1].astype(F32) + orel[h, 1].astype(F32)).astype(BF)
        ocopy[h, "L1"] = send(
            osend.at[h, 0, 1], ofin.at[h, 1, 1], ors.at[h, 5], at_z(3)
        )

    def attend_own(h):
        result = attend(h, (0,))
        num[h] = result[:, :HD]
        tot[h] = result[:, HD:]

    def combine(h):
        for name in ("R0", "R1", "L0", "L1"):
            ocopy[h, name].wait_recv()
        for half in range(2):
            more = ofin[h, 0, half].astype(F32) + ofin[h, 1, half].astype(F32)
            rows = slice(half * BLK, (half + 1) * BLK)
            strip = more[BLK:OROWS]
            total = tot[h, rows, :] + jnp.concatenate([strip] * 16, axis=0).T
            ab[h, 0, rows, :] = ((num[h, rows, :] + more[:BLK]) / total).astype(BF)
            if h == 2:
                part = (top, low)[half]
                own = ab.at[h, 0, part]
                acopy[h, "R", half] = send(own, ab.at[h, 1, part], ars.at[h, half], at_x(1))
                acopy[h, "L", half] = send(own, ab.at[h, 2, part], ars.at[h, 2 + half], at_x(3))
        if h < 2:
            send_ring(ab, acopy, ars, at_x, h)
        both = jnp.dot(ab[h, 0], rs[h * HD : (h + 1) * HD, :], preferred_element_type=F32)
        if h == 0:
            csp[...] = both[:, :HD] + both[:, HD:]
        else:
            csp[...] += both[:, :HD] + both[:, HD:]

    def relay_last():
        acopy[2, "R", 0].wait_recv()
        acopy[2, "RR"] = send(ab.at[2, 1, top], ab.at[2, 3, top], ars.at[2, 4], at_x(1))
        acopy[2, "L", 1].wait_recv()
        acopy[2, "LL"] = send(ab.at[2, 2, low], ab.at[2, 3, low], ars.at[2, 5], at_x(3))

    def send_checks():
        csb[g] = (csp[...] * D ** (-0.5)).T[0:8]
        for k in range(1, 8):
            send(csb.at[g], csb.at[g], crs.at[k], (f, (g + k) % 8))

    def relay_a(h):
        relay_ring(ab, acopy, ars, at_x, h)

    def arrived_a(h):
        arrived_ring(acopy, h)

    def last_rows(half, side):
        part = slice(half * BLK, (half + 1) * BLK)
        rows = jnp.concatenate([ab[2, k, part, :] for k in range(4)], axis=1)
        block = jnp.concatenate([wx[k, side, 2 * HD : COLS, :] for k in range(4)], axis=0)
        return po[side, part, :] + jnp.dot(rows, block, preferred_element_type=F32)

    def project_first():
        for side in range(2):
            total = None
            for k in range(4):
                rows = jnp.concatenate([ab[0, k], ab[1, k]], axis=1)
                part = jnp.dot(rows, wx[k, side, 0 : 2 * HD, :], preferred_element_type=F32)
                total = part if total is None else total + part
            po[side] = total

    def close_checks():
        for k in range(1, 8):
            pltpu.make_async_remote_copy(
                src_ref=csb.at[(g + 8 - k) % 8],
                dst_ref=csb.at[(g + 8 - k) % 8],
                send_sem=pool.at[0],
                recv_sem=crs.at[k],
                device_id=(f, (g + k) % 8),
                device_id_type=MESH,
            ).wait_recv()
        checks = csb[0]
        for k in range(1, 8):
            checks = checks + csb[k]
        cs_ref[...] = checks[0]

    def drain(count):
        for i in range(count):
            sent(i)

    def finish():
        other = (c + zl + 1) % 2
        zcopy = []
        for half in range(2):
            if half == 0:
                acopy[2, "L", 0].wait_recv()
                acopy[2, "RR"].wait_recv()
            else:
                acopy[2, "R", 1].wait_recv()
                acopy[2, "LL"].wait_recv()
            part = (top, low)[half]
            zs[part, :] = last_rows(half, other).astype(BF)
            zcopy.append(send(zs.at[part], zr.at[part], zrs.at[half], zlo))
        kept = [last_rows(half, 1 - other) for half in range(2)]
        drain(len(started) - 2)
        for half in range(2):
            rows = slice(half * BLK, (half + 1) * BLK)
            zcopy[half].wait_recv()
            out_ref[rows, :] = (kept[half] + zr[rows, :].astype(F32)).astype(BF)

    make_first()
    pl.semaphore_wait(barrier, len(peers))
    send_t()
    send_kv(0)
    make_q()
    send_q(0)
    make_rest()
    send_q(1)
    send_q(2)
    make_kv(1)
    send_kv(1)
    make_kv(2)
    for copy in wx_in:
        copy.wait()
    send_w()
    relay_t()
    relay_kv(0)
    send_kv(2)
    row_sums()
    last_kv(0)
    relay_kv(1)
    relay_q(0)
    relay_q(1)
    limits_table()
    arrived_kv(0)
    attend_sides(0)
    relay_kv(2)
    relay_q(2)
    last_kv(1)
    arrived_q(0)
    attend_opp(0)
    early = len(started)
    arrived_kv(1)
    attend_sides(1)
    last_kv(2)
    arrived_q(1)
    attend_opp(1)
    relay_o(0)
    arrived_kv(2)
    arrived_q(2)
    attend_opp(2)
    attend_own(0)
    attend_sides(2)
    relay_o(1)
    share_w()
    attend_own(1)
    attend_own(2)
    combine(0)
    relay_o(2)
    drain(early)
    arrived_w()
    combine(1)
    relay_a(0)
    combine(2)
    send_checks()
    relay_a(1)
    relay_last()
    arrived_a(0)
    arrived_a(1)
    project_first()
    close_checks()
    finish()
    drain(len(started))


def layer_kernel(*refs):
    dma = pltpu.SemaphoreType.DMA
    shapes = ((POOL,), (HL, 8), (HL, 4), (3,), (7,), (HL, 6), (HL, 6), (2,), (8,))
    pl.run_scoped(lambda *sems: layer_body(*sems, *refs), *(dma(shape) for shape in shapes))


def place_kernel(rows_ref, sums_ref, rows_hbm, sums_hbm, sem):
    copies = [
        pltpu.make_async_copy(rows_ref, rows_hbm, sem.at[0]),
        pltpu.make_async_copy(sums_ref, sums_hbm, sem.at[1]),
    ]
    for copy in copies:
        copy.start()
    for copy in copies:
        copy.wait()


def per_device(tokens, w_qkv, norm_gains, w_out, near_mask, far_pattern, window):
    any_spec = pl.BlockSpec(memory_space=pl.ANY)
    vmem_spec = pl.BlockSpec(memory_space=pltpu.VMEM)
    dma = pltpu.SemaphoreType.DMA
    held = pl.pallas_call(
        layer_kernel,
        name="layer",
        out_shape=(
            pltpu.VMEM((SLAB, COLS), BF),
            pltpu.VMEM((SLAB,), F32),
        ),
        in_specs=[any_spec] * 7,
        out_specs=(vmem_spec, vmem_spec),
        scratch_shapes=[
            pltpu.VMEM((SLAB, D), BF),
            pltpu.VMEM((HL, D, 2 * HD), BF),
            pltpu.VMEM((D, COLS), BF),
            pltpu.VMEM((4, 2, COLS, COLS), BF),
            pltpu.VMEM((COLS, D), BF),
            pltpu.VMEM((COLS, 2 * HD), BF),
            pltpu.VMEM((SLAB, HD), F32),
            pltpu.VMEM((HL, 8, SLAB, 2 * HD), BF),
            pltpu.VMEM((HL, 4, SLAB, HD), BF),
            pltpu.VMEM((2, COLS), F32),
            pltpu.SMEM((2, 4), jnp.int32),
            pltpu.VMEM((2, 64), jnp.int32),
            pltpu.SMEM((32,), jnp.int32),
            pltpu.VMEM((8, 128), jnp.int32),
            pltpu.VMEM((4, 8, 128), F32),
            pltpu.VMEM((8, 32, SLAB), F32),
            pltpu.VMEM((2, BLK, SLAB), F32),
            pltpu.VMEM((2 * SLAB, 8 * SLAB), BF),
            pltpu.VMEM((2 * SLAB, 2 * HD), F32),
            pltpu.VMEM((HL, SLAB, HD), F32),
            pltpu.VMEM((HL, SLAB, HD), F32),
            pltpu.VMEM((HL, 3, 2, OROWS, HD), BF),
            pltpu.VMEM((HL, 2, OROWS, HD), BF),
            pltpu.VMEM((HL, 2, 2, OROWS, HD), BF),
            pltpu.VMEM((HL, 4, SLAB, HD), BF),
            pltpu.VMEM((2, SLAB, COLS), F32),
            pltpu.VMEM((SLAB, COLS), BF),
            pltpu.VMEM((SLAB, COLS), BF),
            pltpu.VMEM((8, 8, SLAB), F32),
        ],
        compiler_params=pltpu.CompilerParams(
            collective_id=0, has_side_effects=True, vmem_limit_bytes=56 * 1024 * 1024
        ),
    )(tokens, w_qkv, w_out, norm_gains, near_mask, far_pattern, window)
    return pl.pallas_call(
        place_kernel,
        name="place",
        out_shape=(
            jax.ShapeDtypeStruct((SLAB, COLS), BF),
            jax.ShapeDtypeStruct((SLAB,), F32),
        ),
        in_specs=[vmem_spec, vmem_spec],
        out_specs=(any_spec, any_spec),
        scratch_shapes=[dma((2,))],
    )(*(pltpu.with_memory_space_constraint(part, pltpu.VMEM) for part in held))


def solution(mesh):
    in_specs = (
        P("frame", None),
        P(None, None, "head"),
        P(None, "head"),
        P("head", None),
        P("frame", None),
        P("frame", None),
        P(),
    )
    out_specs = (P("frame", "head"), P("frame"))
    return jax.shard_map(
        per_device, mesh=mesh, in_specs=in_specs, out_specs=out_specs, check_vma=False
    )
```

```python
import jax
import jax.numpy as jnp
from jax import lax
from jax.experimental import pallas as pl
from jax.experimental.pallas import tpu as pltpu
from jax.sharding import PartitionSpec as P

D = 3072
HD = 128
BLK = 128
SLAB = 256
HL = 3
COLS = HL * HD
POOL = 40
PART = 1024
MESH = pl.DeviceIdType.MESH
BF = jnp.bfloat16
F32 = jnp.float32
LOG2E = 1.4426950408889634
OROWS = BLK + 8
NT = (((1,), (1,)), ((), ()))


def layer_body(
    pool,
    krs,
    qrs,
    trs,
    wrs,
    ors,
    ars,
    zrs,
    crs,
    tok_hbm,
    w_hbm,
    wo_hbm,
    gains_hbm,
    near_hbm,
    far_hbm,
    window_hbm,
    out_ref,
    cs_ref,
    tok,
    wkv,
    wq,
    wx,
    wo,
    rs,
    csp,
    kv,
    qb,
    gains_ref,
    near_ref,
    far_ref,
    window_ref,
    far,
    tbuf,
    texp,
    dist,
    pbuf,
    acc,
    num,
    tot,
    osend,
    orel,
    ofin,
    ab,
    po,
    zs,
    zr,
    csb,
):
    f = lax.axis_index("frame")
    g = lax.axis_index("head")
    zh, y, c = f // 8, (f // 2) % 4, f % 2
    zl, x = g // 4, g % 4

    def at_y(step):
        return (zh * 8 + ((y + step) % 4) * 2 + c, g)

    def at_z(step):
        return (((zh + step) % 4) * 8 + y * 2 + c, g)

    def at_x(step):
        return (f, zl * 4 + (x + step) % 4)

    core = (zh * 8 + y * 2 + (1 - c), g)
    zlo = (f, (1 - zl) * 4 + x)

    started = []
    waited = set()

    def sent(i):
        if i not in waited:
            waited.add(i)
            started[i].wait_send()

    def send(src, dst, rsem, dev):
        n = len(started)
        if n >= POOL:
            sent(n - POOL)
        copy = pltpu.make_async_remote_copy(
            src_ref=src,
            dst_ref=dst,
            send_sem=pool.at[n % POOL],
            recv_sem=rsem,
            device_id=dev,
            device_id_type=MESH,
        )
        copy.start()
        started.append(copy)
        return copy

    def fetch(src, dst, i):
        copy = pltpu.make_async_copy(src, dst, pool.at[POOL - 22 + i])
        copy.start()
        return copy

    def columns(side, step):
        at = (side * 4 + (x + step) % 4) * COLS
        return pl.ds(pl.multiple_of(at, HD), COLS)

    small_in = [
        fetch(near_hbm, near_ref, 10),
        fetch(window_hbm, window_ref, 11),
        fetch(far_hbm, far_ref, 12),
        fetch(gains_hbm, gains_ref, 13),
    ]
    kv_in = []
    for k in range(3):
        span = pl.ds(k * PART, PART)
        kv_in.append(
            (
                fetch(tok_hbm.at[:, span], tok.at[:, span], 3 * k),
                fetch(w_hbm.at[1, span, pl.ds(0, HD)], wkv.at[0, span, pl.ds(0, HD)], 3 * k + 1),
                fetch(w_hbm.at[2, span, pl.ds(0, HD)], wkv.at[0, span, pl.ds(HD, HD)], 3 * k + 2),
            )
        )
    barrier = pltpu.get_barrier_semaphore()
    peers = [at_y(1), at_y(3), core, at_z(1), at_z(3)]
    peers += [(f, (g + k) % 8) for k in range(1, 8)]
    for peer in peers:
        pl.semaphore_signal(barrier, inc=1, device_id=peer, device_id_type=MESH)

    first, rest = pl.ds(0, HD), pl.ds(HD, 2 * HD)
    q_first = fetch(w_hbm.at[0, :, first], wq.at[:, first], 14)
    q_rest = fetch(w_hbm.at[0, :, rest], wq.at[:, rest], 15)
    later_in = {}
    for h in (1, 2):
        hs = pl.ds(h * HD, HD)
        later_in[h] = (
            fetch(w_hbm.at[1, :, hs], wkv.at[h, :, pl.ds(0, HD)], 14 + 2 * h),
            fetch(w_hbm.at[2, :, hs], wkv.at[h, :, pl.ds(HD, HD)], 15 + 2 * h),
        )
    wx_in = (
        fetch(wo_hbm.at[:, columns(c, 0)], wx.at[0, 0], 9),
        fetch(wo_hbm.at[:, columns(1 - c, 0)], wx.at[0, 1], 20),
        fetch(wo_hbm, wo, 21),
    )

    for copy in small_in:
        copy.wait()
    lane = lax.broadcasted_iota(jnp.int32, (8, 128), 1)
    line = lax.broadcasted_iota(jnp.int32, (8, 128), 0)
    slabs = lax.shift_right_logical(lane, 1)
    odd = lane - 2 * slabs
    apart = jnp.abs(slabs - f)
    limits = jnp.zeros((8, 128), jnp.int32)
    for d in range(32):
        limits = jnp.where(apart == d, window_ref[d], limits)
    near = []
    for a in range(2):
        before = jnp.where(odd == 1, near_ref[a, 1], near_ref[a, 0])
        after = jnp.where(odd == 1, near_ref[a, 3], near_ref[a, 2])
        near.append(jnp.where(slabs < f, before, after))
    far[...] = jnp.zeros((8, 128), jnp.int32)
    far[0:2, 0:64] = far_ref[...]
    chosen = jnp.where(apart == 1, jnp.where(line == 0, near[0], near[1]), far[...])
    chosen = jnp.where(apart == 0, 1, chosen)
    tbuf[0] = jnp.where(chosen > 0, limits, 0).astype(F32)

    def keep_kv(h, both):
        key = both[:, :HD]
        factor = lax.rsqrt(jnp.mean(key * key, axis=1, keepdims=True) + 1e-06)
        gain = gains_ref[1:2, h * HD : (h + 1) * HD]
        kv[h, 0, :, 0:HD] = (key * factor * gain).astype(BF)
        kv[h, 0, :, HD : 2 * HD] = both[:, HD:].astype(BF)

    def make_first():
        both = None
        for k in range(3):
            for copy in kv_in[k]:
                copy.wait()
            span = slice(k * PART, (k + 1) * PART)
            part = jnp.dot(tok[:, span], wkv[0, span, :], preferred_element_type=F32)
            both = part if both is None else both + part
        keep_kv(0, both)

    def make_kv(h):
        for copy in later_in[h]:
            copy.wait()
        keep_kv(h, jnp.dot(tok[...], wkv[h], preferred_element_type=F32))

    def keep_q(h, query):
        factor = lax.rsqrt(jnp.mean(query * query, axis=1, keepdims=True) + 1e-06)
        gain = gains_ref[0:1, h * HD : (h + 1) * HD] * (HD**-0.5 * LOG2E)
        qb[h, 0] = (query * factor * gain).astype(BF)

    def make_q():
        q_first.wait()
        keep_q(0, jnp.dot(tok[...], wq[:, 0:HD], preferred_element_type=F32))

    def make_rest():
        q_rest.wait()
        both = jnp.dot(tok[...], wq[:, HD:], preferred_element_type=F32)
        keep_q(1, both[:, :HD])
        keep_q(2, both[:, HD:])

    top, low = pl.ds(0, BLK), pl.ds(BLK, BLK)
    kcopy, qcopy, tcopy, wcopy, ocopy, acopy = {}, {}, {}, {}, {}, {}

    def send_kv(h):
        own = kv.at[h, 0]
        kcopy[h, "R"] = send(own, kv.at[h, 1], krs.at[h, 0], at_y(1))
        kcopy[h, "L"] = send(own, kv.at[h, 2], krs.at[h, 1], at_y(3))
        kcopy[h, "c0"] = send(own, kv.at[h, 4], krs.at[h, 2], core)

    def relay_kv(h):
        kcopy[h, "R"].wait_recv()
        kcopy[h, "RR"] = send(
            kv.at[h, 1, top], kv.at[h, 3, top], krs.at[h, 3], at_y(1)
        )
        kcopy[h, "c1"] = send(kv.at[h, 1], kv.at[h, 5], krs.at[h, 4], core)
        kcopy[h, "L"].wait_recv()
        kcopy[h, "LL"] = send(
            kv.at[h, 2, low], kv.at[h, 3, low], krs.at[h, 5], at_y(3)
        )
        kcopy[h, "c2"] = send(kv.at[h, 2], kv.at[h, 6], krs.at[h, 6], core)

    def last_kv(h):
        kcopy[h, "RR"].wait_recv()
        kcopy[h, "LL"].wait_recv()
        kcopy[h, "c3"] = send(kv.at[h, 3], kv.at[h, 7], krs.at[h, 7], core)

    def arrived_kv(h):
        for name in ("c0", "c1", "c2", "c3"):
            kcopy[h, name].wait_recv()

    def send_ring(buf, copies, rsem, to, h):
        own = buf.at[h, 0]
        copies[h, "R"] = send(own, buf.at[h, 1], rsem.at[h, 0], to(1))
        copies[h, "L"] = send(own, buf.at[h, 2], rsem.at[h, 1], to(3))

    def relay_ring(buf, copies, rsem, to, h):
        copies[h, "R"].wait_recv()
        copies[h, "RR"] = send(
            buf.at[h, 1, top], buf.at[h, 3, top], rsem.at[h, 2], to(1)
        )
        copies[h, "L"].wait_recv()
        copies[h, "LL"] = send(
            buf.at[h, 2, low], buf.at[h, 3, low], rsem.at[h, 3], to(3)
        )

    def arrived_ring(copies, h):
        copies[h, "RR"].wait_recv()
        copies[h, "LL"].wait_recv()

    def send_q(h):
        send_ring(qb, qcopy, qrs, at_z, h)

    def relay_q(h):
        relay_ring(qb, qcopy, qrs, at_z, h)

    def arrived_q(h):
        arrived_ring(qcopy, h)

    def send_t():
        tcopy["R"] = send(tbuf.at[0], tbuf.at[1], trs.at[0], at_z(1))
        tcopy["L"] = send(tbuf.at[0], tbuf.at[2], trs.at[1], at_z(3))

    def relay_t():
        tcopy["R"].wait_recv()
        tcopy["RR"] = send(tbuf.at[1], tbuf.at[3], trs.at[2], at_z(1))
        tcopy["L"].wait_recv()

    def send_w():
        for k, step in ((1, 1), (2, 3), (3, 2)):
            wcopy[k] = send(
                wo_hbm.at[:, columns(c, step)], wx.at[k, 0], wrs.at[k], at_x(step)
            )

    def share_w():
        for k in (1, 2, 3):
            wcopy[k].wait_recv()
            wcopy[k + 3] = send(wx.at[k, 0], wx.at[k, 1], wrs.at[k + 3], core)

    def arrived_w():
        for k in (4, 5, 6):
            wcopy[k].wait_recv()

    def limits_table():
        row = lax.broadcasted_iota(jnp.int32, (BLK, SLAB), 0)
        col = lax.broadcasted_iota(jnp.int32, (BLK, SLAB), 1)
        for rh in range(2):
            dist[rh] = jnp.abs(row + rh * BLK - col).astype(F32)
        tcopy["RR"].wait_recv()
        table = tbuf[...].reshape(4 * 8, 128).astype(BF)
        half = (col >= BLK).astype(jnp.int32)
        for j in range(8):
            slab = zh * 8 + ((y + (0, 3, 1, 2)[j % 4]) % 4) * 2 + (c if j < 4 else 1 - c)
            pick = (row == half + slab * 2).astype(F32).astype(BF)
            texp[j] = jnp.dot(table, pick, preferred_element_type=F32)

    def row_sums():
        whole = jnp.dot(wo[...], jnp.ones((D, HD), BF), preferred_element_type=F32)
        high = whole.astype(BF)
        rs[:, 0:HD] = high
        rs[:, HD:] = (whole - high.astype(F32)).astype(BF)

    def attend(h, slots):
        size = SLAB * len(slots)
        queries = jnp.concatenate([qb[h, q] for q in slots], axis=0)

        for k in range(4):
            pair = slice(2 * k, 2 * k + 2)
            cols = slice(2 * k * SLAB, (2 * k + 2) * SLAB)
            for j in range(2 * k, 2 * k + 2):
                raw = lax.dot_general(queries, kv[h, j, :, 0:HD], NT, preferred_element_type=F32)
                for i, q in enumerate(slots):
                    for rh in range(2):
                        rows = slice(i * SLAB + rh * BLK, i * SLAB + (rh + 1) * BLK)
                        limit = texp[j, q * 8 + rh : q * 8 + rh + 1, :]
                        weight = jnp.where(dist[rh] < limit, jnp.exp2(raw[rows]), 0.0)
                        pbuf[rows, j * SLAB : (j + 1) * SLAB] = weight.astype(BF)
            values = kv[h, pair, :, HD : 2 * HD].reshape(2 * SLAB, HD)
            values = jnp.concatenate([values, jnp.ones((2 * SLAB, HD), BF)], axis=1)
            part = jnp.dot(pbuf[0:size, cols], values, preferred_element_type=F32)
            if k == 0:
                acc[0:size, :] = part
            else:
                acc[0:size, :] += part
        return acc[0:size, :]

    def pack(h, dest, part):
        for half in range(2):
            rows = part[half * BLK : (half + 1) * BLK]
            osend[h, dest, half, 0:BLK, :] = rows[:, :HD].astype(BF)
            osend[h, dest, half, BLK:OROWS, :] = rows[:, HD:].T[0:8].astype(BF)

    def attend_opp(h):
        pack(h, 2, attend(h, (3,)))
        ocopy[h, "RR"] = send(
            osend.at[h, 2, 0], orel.at[h, 0], ors.at[h, 0], at_z(1)
        )
        ocopy[h, "LL"] = send(
            osend.at[h, 2, 1], orel.at[h, 1], ors.at[h, 1], at_z(3)
        )

    def attend_sides(h):
        result = attend(h, (1, 2))
        pack(h, 0, result[:SLAB])
        pack(h, 1, result[SLAB:])
        ocopy[h, "R1"] = send(
            osend.at[h, 1, 1], ofin.at[h, 0, 1], ors.at[h, 2], at_z(1)
        )
        ocopy[h, "L0"] = send(
            osend.at[h, 0, 0], ofin.at[h, 1, 0], ors.at[h, 3], at_z(3)
        )

    def relay_o(h):
        ocopy[h, "RR"].wait_recv()
        osend[h, 1, 0] = (osend[h, 1, 0].astype(F32) + orel[h, 0].astype(F32)).astype(BF)
        ocopy[h, "R0"] = send(
            osend.at[h, 1, 0], ofin.at[h, 0, 0], ors.at[h, 4], at_z(1)
        )
        ocopy[h, "LL"].wait_recv()
        osend[h, 0, 1] = (osend[h, 0, 1].astype(F32) + orel[h, 1].astype(F32)).astype(BF)
        ocopy[h, "L1"] = send(
            osend.at[h, 0, 1], ofin.at[h, 1, 1], ors.at[h, 5], at_z(3)
        )

    def attend_own(h):
        result = attend(h, (0,))
        num[h] = result[:, :HD]
        tot[h] = result[:, HD:]

    def combine(h):
        for name in ("R0", "R1", "L0", "L1"):
            ocopy[h, name].wait_recv()
        for half in range(2):
            more = ofin[h, 0, half].astype(F32) + ofin[h, 1, half].astype(F32)
            rows = slice(half * BLK, (half + 1) * BLK)
            strip = more[BLK:OROWS]
            total = tot[h, rows, :] + jnp.concatenate([strip] * 16, axis=0).T
            ab[h, 0, rows, :] = ((num[h, rows, :] + more[:BLK]) / total).astype(BF)
            if h == 2:
                part = (top, low)[half]
                own = ab.at[h, 0, part]
                acopy[h, "R", half] = send(own, ab.at[h, 1, part], ars.at[h, half], at_x(1))
                acopy[h, "L", half] = send(own, ab.at[h, 2, part], ars.at[h, 2 + half], at_x(3))
        if h < 2:
            send_ring(ab, acopy, ars, at_x, h)
        both = jnp.dot(ab[h, 0], rs[h * HD : (h + 1) * HD, :], preferred_element_type=F32)
        if h == 0:
            csp[...] = both[:, :HD] + both[:, HD:]
        else:
            csp[...] += both[:, :HD] + both[:, HD:]

    def relay_last():
        acopy[2, "R", 0].wait_recv()
        acopy[2, "RR"] = send(ab.at[2, 1, top], ab.at[2, 3, top], ars.at[2, 4], at_x(1))
        acopy[2, "L", 1].wait_recv()
        acopy[2, "LL"] = send(ab.at[2, 2, low], ab.at[2, 3, low], ars.at[2, 5], at_x(3))

    def send_checks():
        csb[g] = (csp[...] * D ** (-0.5)).T[0:8]
        for k in range(1, 8):
            send(csb.at[g], csb.at[g], crs.at[k], (f, (g + k) % 8))

    def relay_a(h):
        relay_ring(ab, acopy, ars, at_x, h)

    def arrived_a(h):
        arrived_ring(acopy, h)

    def last_rows(half, side):
        part = slice(half * BLK, (half + 1) * BLK)
        rows = jnp.concatenate([ab[2, k, part, :] for k in range(4)], axis=1)
        block = jnp.concatenate([wx[k, side, 2 * HD : COLS, :] for k in range(4)], axis=0)
        return po[side, part, :] + jnp.dot(rows, block, preferred_element_type=F32)

    def project(h):
        span = slice(h * HD, (h + 1) * HD)
        rows = jnp.concatenate([ab[h, k] for k in range(4)], axis=1)
        for side in range(2):
            block = jnp.concatenate([wx[k, side, span, :] for k in range(4)], axis=0)
            part = jnp.dot(rows, block, preferred_element_type=F32)
            po[side] = part if h == 0 else po[side] + part

    def close_checks():
        for k in range(1, 8):
            pltpu.make_async_remote_copy(
                src_ref=csb.at[(g + 8 - k) % 8],
                dst_ref=csb.at[(g + 8 - k) % 8],
                send_sem=pool.at[0],
                recv_sem=crs.at[k],
                device_id=(f, (g + k) % 8),
                device_id_type=MESH,
            ).wait_recv()
        checks = csb[0]
        for k in range(1, 8):
            checks = checks + csb[k]
        cs_ref[...] = checks[0]

    def drain(count):
        for i in range(count):
            sent(i)

    def finish():
        other = (c + zl + 1) % 2
        zcopy = []
        for half in range(2):
            if half == 0:
                acopy[2, "L", 0].wait_recv()
                acopy[2, "RR"].wait_recv()
            else:
                acopy[2, "R", 1].wait_recv()
                acopy[2, "LL"].wait_recv()
            part = (top, low)[half]
            zs[part, :] = last_rows(half, other).astype(BF)
            zcopy.append(send(zs.at[part], zr.at[part], zrs.at[half], zlo))
        kept = [last_rows(half, 1 - other) for half in range(2)]
        drain(len(started) - 2)
        for half in range(2):
            rows = slice(half * BLK, (half + 1) * BLK)
            zcopy[half].wait_recv()
            out_ref[rows, :] = (kept[half] + zr[rows, :].astype(F32)).astype(BF)

    make_first()
    pl.semaphore_wait(barrier, len(peers))
    send_t()
    send_kv(0)
    make_q()
    send_q(0)
    make_rest()
    send_q(1)
    send_q(2)
    make_kv(1)
    send_kv(1)
    make_kv(2)
    for copy in wx_in:
        copy.wait()
    send_w()
    relay_t()
    relay_kv(0)
    send_kv(2)
    row_sums()
    last_kv(0)
    relay_kv(1)
    relay_q(0)
    relay_q(1)
    limits_table()
    arrived_kv(0)
    attend_sides(0)
    relay_kv(2)
    relay_q(2)
    last_kv(1)
    arrived_q(0)
    attend_opp(0)
    early = len(started)
    arrived_kv(1)
    attend_sides(1)
    last_kv(2)
    arrived_q(1)
    attend_opp(1)
    relay_o(0)
    arrived_kv(2)
    arrived_q(2)
    attend_opp(2)
    attend_own(0)
    attend_sides(2)
    relay_o(1)
    share_w()
    attend_own(1)
    attend_own(2)
    combine(0)
    relay_o(2)
    drain(early)
    arrived_w()
    combine(1)
    relay_a(0)
    combine(2)
    send_checks()
    relay_a(1)
    relay_last()
    arrived_a(0)
    project(0)
    arrived_a(1)
    project(1)
    close_checks()
    finish()
    drain(len(started))


def layer_kernel(*refs):
    dma = pltpu.SemaphoreType.DMA
    shapes = ((POOL,), (HL, 8), (HL, 4), (3,), (7,), (HL, 6), (HL, 6), (2,), (8,))
    pl.run_scoped(lambda *sems: layer_body(*sems, *refs), *(dma(shape) for shape in shapes))


def place_kernel(rows_ref, sums_ref, rows_hbm, sums_hbm, sem):
    copies = [
        pltpu.make_async_copy(rows_ref, rows_hbm, sem.at[0]),
        pltpu.make_async_copy(sums_ref, sums_hbm, sem.at[1]),
    ]
    for copy in copies:
        copy.start()
    for copy in copies:
        copy.wait()


def per_device(tokens, w_qkv, norm_gains, w_out, near_mask, far_pattern, window):
    any_spec = pl.BlockSpec(memory_space=pl.ANY)
    vmem_spec = pl.BlockSpec(memory_space=pltpu.VMEM)
    dma = pltpu.SemaphoreType.DMA
    held = pl.pallas_call(
        layer_kernel,
        name="layer",
        out_shape=(
            pltpu.VMEM((SLAB, COLS), BF),
            pltpu.VMEM((SLAB,), F32),
        ),
        in_specs=[any_spec] * 7,
        out_specs=(vmem_spec, vmem_spec),
        scratch_shapes=[
            pltpu.VMEM((SLAB, D), BF),
            pltpu.VMEM((HL, D, 2 * HD), BF),
            pltpu.VMEM((D, COLS), BF),
            pltpu.VMEM((4, 2, COLS, COLS), BF),
            pltpu.VMEM((COLS, D), BF),
            pltpu.VMEM((COLS, 2 * HD), BF),
            pltpu.VMEM((SLAB, HD), F32),
            pltpu.VMEM((HL, 8, SLAB, 2 * HD), BF),
            pltpu.VMEM((HL, 4, SLAB, HD), BF),
            pltpu.VMEM((2, COLS), F32),
            pltpu.SMEM((2, 4), jnp.int32),
            pltpu.VMEM((2, 64), jnp.int32),
            pltpu.SMEM((32,), jnp.int32),
            pltpu.VMEM((8, 128), jnp.int32),
            pltpu.VMEM((4, 8, 128), F32),
            pltpu.VMEM((8, 32, SLAB), F32),
            pltpu.VMEM((2, BLK, SLAB), F32),
            pltpu.VMEM((2 * SLAB, 8 * SLAB), BF),
            pltpu.VMEM((2 * SLAB, 2 * HD), F32),
            pltpu.VMEM((HL, SLAB, HD), F32),
            pltpu.VMEM((HL, SLAB, HD), F32),
            pltpu.VMEM((HL, 3, 2, OROWS, HD), BF),
            pltpu.VMEM((HL, 2, OROWS, HD), BF),
            pltpu.VMEM((HL, 2, 2, OROWS, HD), BF),
            pltpu.VMEM((HL, 4, SLAB, HD), BF),
            pltpu.VMEM((2, SLAB, COLS), F32),
            pltpu.VMEM((SLAB, COLS), BF),
            pltpu.VMEM((SLAB, COLS), BF),
            pltpu.VMEM((8, 8, SLAB), F32),
        ],
        compiler_params=pltpu.CompilerParams(
            collective_id=0, has_side_effects=True, vmem_limit_bytes=56 * 1024 * 1024
        ),
    )(tokens, w_qkv, w_out, norm_gains, near_mask, far_pattern, window)
    return pl.pallas_call(
        place_kernel,
        name="place",
        out_shape=(
            jax.ShapeDtypeStruct((SLAB, COLS), BF),
            jax.ShapeDtypeStruct((SLAB,), F32),
        ),
        in_specs=[vmem_spec, vmem_spec],
        out_specs=(any_spec, any_spec),
        scratch_shapes=[dma((2,))],
    )(*(pltpu.with_memory_space_constraint(part, pltpu.VMEM) for part in held))


def solution(mesh):
    in_specs = (
        P("frame", None),
        P(None, None, "head"),
        P(None, "head"),
        P("head", None),
        P("frame", None),
        P("frame", None),
        P(),
    )
    out_specs = (P("frame", "head"), P("frame"))
    return jax.shard_map(
        per_device, mesh=mesh, in_specs=in_specs, out_specs=out_specs, check_vma=False
    )
```
